32 devices in a mesh: scen: 2 (over y), site: 4 (over z), sub: 2 (over x), var: 2 (over core).
Axes of the slice: x: 2, y: 2, z: 4, core: 2. Of those that a mesh axis runs over, the one named last changes fastest.
Arguments:
- green_tensor: bfloat16 [8, 2, 16, 2, 2, 3, 32, 6, 128], P(('scen', 'site'), 'sub', None, 'var'), parts along dimension 0, may hold values from -0.078125 to 0.078125
- rupture_spectra: bfloat16 [2, 2, 512, 6, 1024], P(None, None, ('scen', 'var'), None, ('sub', 'site')), parts along dimension 2, may hold values from -6 to 6
- pair_site: int32 [8, 2, 16], P(('scen', 'site'), 'sub'), parts along dimension 0, may hold values from 0 to 3, as said below
- pair_block: int32 [8, 2, 16], P(('scen', 'site'), 'sub'), parts along dimension 0, may hold values from 0 to 3, as said below
- pair_count: int32 [8, 2, 16], P(('scen', 'site'), 'sub'), parts along dimension 0, may hold values from 0 to 128, as said below
- band_offset: int32 [2], P('scen'), parts along dimension 0, may hold values from 0 to 127
Outputs:
- site_spectra: float32 [2, 2, 3, 256, 1024], P(None, None, None, 'var', ('scen', 'site', 'sub')), parts along dimension 4
The draws below stay inside these ranges and needn't reach their ends.
There are 2 independent parts, one for each index of `scen`. The reference program is written for one: setup_inputs(seed, part) draws one part's arguments, and reference() takes and returns one part's arrays. A program takes and returns all parts, laid end to end along the dimension named above; each array names one. Nothing has to cross between parts.
Inputs may be any that keep to these rules, and one draw needn't show every extreme that they name: On each device the live slots come first and are followed by unused slots; live slots name distinct pairs; unused slots have pair_count 0. No device has more than 12 live slots, and some device of every draw has exactly 12. `pair_site`: site block within the device's 4 site blocks. `pair_block`: subfault block within the device's group of 4 blocks.
All inputs are finite; a program needn't handle non-finite values.
Results may differ from the reference program's by a relative error of at most 0.0003.
Values may be sent and summed in bfloat16 or wider, within the bound.
No kernel may reach another device: no remote copies, remote signals or barrier semaphores. Data moves between devices by JAX's collectives and lax.ppermute only.
A program may use at most 64 MiB of HBM per device.

```python
import jax
import jax.numpy as jnp
from jax import lax

FREQS = 2
VARIATIONS = 256
BLOCK_SITES = 32
SITE_BLOCKS = 4
SUB_BLOCKS = 4
PAIRS = 16
LIVE_MOST = 12
SITES = 512
SUBFAULTS = 1024
N_SITE = 4
N_SUB = 2


def pair_tables(key):
    base = jax.random.fold_in(key, 7)
    key_live, key_full, key_order, key_whole, key_part = jax.random.split(base, 5)
    devices_count = N_SITE * N_SUB
    combos = SITE_BLOCKS * SUB_BLOCKS
    live = jax.random.randint(key_live, (devices_count,), 1, LIVE_MOST + 1)
    chosen = jax.random.randint(key_full, (), 0, devices_count)
    live = jnp.where(jnp.arange(devices_count) == chosen, LIVE_MOST, live)
    scores = jax.random.randint(key_order, (devices_count, combos), 0, 2 ** 20) * combos + jnp.arange(combos)[None, :]
    order = jnp.argsort(scores, axis=1)[:, :PAIRS].astype(jnp.int32)
    sites = order // SUB_BLOCKS
    blocks = order % SUB_BLOCKS
    whole_flag = jax.random.randint(key_whole, (devices_count, PAIRS), 0, 4)
    partial_value = jax.random.randint(key_part, (devices_count, PAIRS), 1, 128)
    counts = jnp.where(whole_flag > 0, 128, partial_value)
    slot_index = jnp.arange(PAIRS)[None, :]
    counts = jnp.where(slot_index < live[:, None], counts, 0)
    shape = (N_SITE, N_SUB, PAIRS)
    return (sites.reshape(shape).astype(jnp.int32), blocks.reshape(shape).astype(jnp.int32), counts.reshape(shape).astype(jnp.int32))


def draw_pair_site(key, part):
    return pair_tables(key)[0]


def draw_pair_block(key, part):
    return pair_tables(key)[1]


def draw_pair_count(key, part):
    return pair_tables(key)[2]


def block_levels(own_key, extent, cuts, smallest, high):
    def one(axis_at, shards_of):
        steps = jax.random.uniform(jax.random.fold_in(jax.random.fold_in(own_key, 6), axis_at), (shards_of,), jnp.float32, smallest / len(cuts), high / len(cuts))
        return jnp.repeat(jnp.exp(steps), extent[axis_at] // shards_of).reshape((-1,) + (1,) * (len(extent) - axis_at - 1))

    loudness = one(*cuts[0])
    for cut in cuts[1:]:
        loudness = loudness * one(*cut)
    return loudness


def centred(own_key, extent, deviation, bound, cuts=(), kind=jnp.bfloat16):
    result = deviation * jax.random.normal(own_key, extent, jnp.float32)
    if cuts:
        result = result * block_levels(own_key, extent, cuts, -0.22, 0.18)
    return jnp.clip(result, -bound, bound).astype(kind)


def setup_inputs(seed: int = 0, part: int = 0) -> dict:
    streams_of = jax.random.split(jax.random.key(seed), 7)
    part_keys = jax.random.split(jax.random.fold_in(streams_of[6], part), 7)
    return {
        "green_tensor": centred(part_keys[0], (N_SITE, N_SUB, PAIRS, FREQS, 2, 3, BLOCK_SITES, 6, 128), (6 * 128 * N_SUB * PAIRS // SITE_BLOCKS) ** -0.5, 0.078125, ((0, 4), (1, 2), (3, 2))),
        "rupture_spectra": centred(part_keys[1], (FREQS, 2, VARIATIONS, 6, SUBFAULTS), 1.0, 6.0, ((2, 2), (4, 8))),
        "pair_site": draw_pair_site(jax.random.fold_in(jax.random.fold_in(streams_of[6], part), 71), part),
        "pair_block": draw_pair_block(jax.random.fold_in(jax.random.fold_in(streams_of[6], part), 71), part),
        "pair_count": draw_pair_count(jax.random.fold_in(jax.random.fold_in(streams_of[6], part), 71), part),
        "band_offset": jax.random.randint(part_keys[5], (1,), 0, 128).astype(jnp.int32),
    }


CORNER = 48.0


def reference(green_tensor, rupture_spectra, pair_site, pair_block, pair_count, band_offset):
    total_slots = N_SITE * N_SUB * PAIRS
    tiles = green_tensor.reshape((total_slots, FREQS, 2, 3, BLOCK_SITES, 6, 128))
    owner_rank = jnp.arange(total_slots, dtype=jnp.int32) // PAIRS
    site_rank = owner_rank // N_SUB
    group_rank = owner_rank % N_SUB
    global_site = (site_rank * SITE_BLOCKS + pair_site.reshape(-1)).astype(jnp.int32)
    global_block = (group_rank * SUB_BLOCKS + pair_block.reshape(-1)).astype(jnp.int32)
    counts = pair_count.reshape(-1).astype(jnp.int32)
    columns = jnp.arange(128, dtype=jnp.int32)
    totals = jnp.zeros((FREQS, 2, 3, VARIATIONS, SITES), jnp.float32)

    def live_pair(totals, tensor_tile, site_block, sub_block, live_count):
        spectrum = lax.dynamic_slice_in_dim(rupture_spectra, sub_block * 128, 128, axis=4).astype(jnp.float32)
        keep_mask = (columns < live_count).astype(jnp.float32)
        spectrum = spectrum * keep_mask
        products = jnp.einsum("fpcsmk,fqvmk->fpqcvs", tensor_tile.astype(jnp.float32), spectrum,
                              precision=lax.Precision.HIGHEST)
        real_part = products[:, 0, 0] - products[:, 1, 1]
        imag_part = products[:, 0, 1] + products[:, 1, 0]
        contrib = jnp.stack([real_part, imag_part], axis=1)
        corner = (jnp.int32(0), jnp.int32(0), jnp.int32(0), jnp.int32(0), (site_block * BLOCK_SITES).astype(jnp.int32))
        current = lax.dynamic_slice(totals, corner, contrib.shape)
        return lax.dynamic_update_slice(totals, current + contrib, corner)

    def add_pair(totals, item):
        tensor_tile, site_block, sub_block, live_count = item
        totals = lax.cond(live_count > 0,
                          lambda acc: live_pair(acc, tensor_tile, site_block, sub_block, live_count),
                          lambda acc: acc, totals)
        return totals, None

    totals, _ = lax.scan(add_pair, totals, (tiles, global_site, global_block, counts))
    freq_index = (band_offset[0] + jnp.arange(FREQS, dtype=jnp.int32)).astype(jnp.float32)
    brune = 1.0 / (1.0 + (freq_index / CORNER) ** 2)
    return totals * brune[:, None, None, None, None]
```

```python
import functools

import jax
import jax.numpy as jnp
from jax import lax
from jax.experimental import pallas as pl
from jax.experimental.pallas import tpu as pltpu
from jax.sharding import PartitionSpec as P

FREQS = 2
SITE_BLOCKS = 4
SUB_BLOCKS = 4
CORNER = 48.0


def place_of(block, z):
    flip = z >= 2
    block = jnp.where(flip, 3 - block, block)
    z = jnp.where(flip, 3 - z, z)
    return jnp.where(block < 2, block ^ z, block)


def pair_kernel(lo, hi, last, line, freq, *refs):
    refs = list(refs)
    ids, site_t, block_t, count_t = refs[:4]
    refs = refs[4:]
    g_own, g_other = refs[:2]
    refs = refs[2:]
    n = hi - lo
    sources = []
    for place in range(lo, hi):
        if line and place >= 2:
            sources.append(refs[:2])
            refs = refs[2:]
        else:
            sources.append(refs[:1])
            refs = refs[1:]
    acc_in = None
    if lo > 0:
        acc_in = refs.pop(0)
    if last:
        keep, send = refs[:2]
        refs = refs[2:]
    else:
        acc_out = refs.pop(0)
    gbuf, mbuf, counts, gsem, msem = refs
    z, j, v = ids[0], ids[1], ids[2]
    slots = g_own.shape[0]
    middle = jnp.logical_and(z > 0, z < 3)

    for q in range(n):
        srcs = sources[q]
        if len(srcs) == 1:
            pltpu.make_async_copy(srcs[0], mbuf.at[q], msem.at[q]).start()
        else:

            @pl.when(middle)
            def _():
                pltpu.make_async_copy(srcs[0], mbuf.at[q], msem.at[q]).start()

            @pl.when(jnp.logical_not(middle))
            def _():
                pltpu.make_async_copy(srcs[1], mbuf.at[q], msem.at[q]).start()

    for q in range(n):
        for s in range(SITE_BLOCKS):
            counts[q, s] = 0

    def slot_at(p):
        block = block_t[0, 0, p]
        place = place_of(block, z) if line else block
        live = jnp.logical_and(
            count_t[0, 0, p] > 0, jnp.logical_and(place >= lo, place < hi)
        )
        half = SITE_BLOCKS // 2
        s = site_t[0, 0, p]
        row = (s // half ^ j) * half + s % half
        return live, place - lo, row

    def load(p, _):
        live, q, row = slot_at(p)

        @pl.when(live)
        def _():
            counts[q, row] = count_t[0, 0, p]

            @pl.when(v == freq)
            def _():
                pltpu.make_async_copy(
                    g_own.at[p], gbuf.at[q, :, :, :, row], gsem
                ).start()

            @pl.when(v != freq)
            def _():
                pltpu.make_async_copy(
                    g_other.at[p], gbuf.at[q, :, :, :, row], gsem
                ).start()

        return 0

    lax.fori_loop(0, slots, load, 0)

    def drain(p, _):
        live, q, row = slot_at(p)

        @pl.when(live)
        def _():
            pltpu.make_async_copy(g_own.at[p], gbuf.at[q, :, :, :, row], gsem).wait()

        return 0

    lax.fori_loop(0, slots, drain, 0)
    for q in range(n):
        pltpu.make_async_copy(sources[q][0], mbuf.at[q], msem.at[q]).wait()

    moments = gbuf.shape[3]
    block_sites = gbuf.shape[5]
    variants = mbuf.shape[3]
    sites = SITE_BLOCKS * block_sites
    for c in range(3):
        total = None
        for q in range(n):
            lane = lax.broadcasted_iota(jnp.int32, (block_sites, 128), 1)
            pieces = []
            for m in range(moments):
                rows = []
                for r in range(2):
                    for s in range(SITE_BLOCKS):
                        rows.append(
                            jnp.where(
                                lane < counts[q, s],
                                gbuf[q, r, c, m, s],
                                jnp.zeros((), gbuf.dtype),
                            )
                        )
                pieces.append(jnp.concatenate(rows, axis=0))
            lhs = jnp.concatenate(pieces, axis=1)
            rhs = jnp.concatenate(
                [mbuf[q, :, m].reshape(2 * variants, 128) for m in range(moments)],
                axis=1,
            )
            prod = lax.dot_general(
                lhs, rhs, (((1,), (1,)), ((), ())), preferred_element_type=jnp.float32
            )
            total = prod if total is None else total + prod
        real = total[:sites, :variants] - total[sites:, variants:]
        imag = total[:sites, variants:] + total[sites:, :variants]
        for r, value in enumerate((real, imag)):
            if acc_in is not None:
                value = value + acc_in[r, c]
            if last:
                keep[r, c] = value[: sites // 2]
                send[r, c] = value[sites // 2 :]
            else:
                acc_out[r, c] = value


def pair_sums(lo, hi, last, line, freq, ids, tables, tensors, sources, acc=None):
    slots, _, comps, moments, block_sites, columns = tensors[0].shape
    variants = sources[0].shape[2]
    sites = SITE_BLOCKS * block_sites
    n = hi - lo
    smem = pl.BlockSpec(memory_space=pltpu.SMEM)
    hbm = pl.BlockSpec(memory_space=pl.ANY)
    vmem = pl.BlockSpec(memory_space=pltpu.VMEM)
    operands = [ids, *tables, *tensors, *sources]
    in_specs = [smem] * 4 + [hbm] * (2 + len(sources))
    if acc is not None:
        operands.append(acc)
        in_specs.append(vmem)
    if last:
        shape = jax.ShapeDtypeStruct((2, comps, sites // 2, variants), jnp.float32)
        out_shape = (shape, shape)
        out_specs = (vmem, vmem)
    else:
        out_shape = jax.ShapeDtypeStruct((2, comps, sites, variants), jnp.float32)
        out_specs = vmem
    flops = n * 2 * (2 * comps * sites) * (2 * variants) * moments * columns
    return pl.pallas_call(
        functools.partial(pair_kernel, lo, hi, last, line, freq),
        out_shape=out_shape,
        in_specs=in_specs,
        out_specs=out_specs,
        scratch_shapes=[
            pltpu.VMEM(
                (n, 2, comps, moments, SITE_BLOCKS, block_sites, columns),
                tensors[0].dtype,
            ),
            pltpu.VMEM((n, 2, moments, variants, columns), sources[0].dtype),
            pltpu.SMEM((n, SITE_BLOCKS), jnp.int32),
            pltpu.SemaphoreType.DMA,
            pltpu.SemaphoreType.DMA((n,)),
        ],
        compiler_params=pltpu.CompilerParams(vmem_limit_bytes=24 << 20),
        cost_estimate=pl.CostEstimate(
            flops=flops, bytes_accessed=n * 1_600_000, transcendentals=0
        ),
    )(*operands)


def line_steps(own):
    send = functools.partial(lax.ppermute, axis_name="site")
    pairs = send(own, perm=[(0, 1), (1, 0), (2, 3), (3, 2)])
    inner = send(own, perm=[(1, 2), (2, 1)])
    outer = send(inner, perm=[(1, 0), (2, 3)])
    inner_far = send(pairs, perm=[(1, 2), (2, 1)])
    outer_far = send(inner_far, perm=[(1, 0), (2, 3)])
    return pairs, inner, outer, inner_far, outer_far


def shards(n_site, n_sub, tensor, spectra, pair_site, pair_block, pair_count, offset):
    spectra = spectra.transpose(0, 1, 3, 2, 4)
    tensor = tensor[0, 0, :, 0].transpose(0, 1, 2, 4, 3, 5)
    tables = (pair_site, pair_block, pair_count)
    line = n_site == SUB_BLOCKS
    swap = n_sub == 2
    half = lax.axis_index("sub") if swap else 0
    ids = jnp.stack([lax.axis_index("site"), half, lax.axis_index("var")])
    ids = ids.astype(jnp.int32)
    kept, sent = [], []
    if line:
        steps = [line_steps(spectra[f]) for f in range(FREQS)]
    else:
        whole = lax.all_gather(spectra, "site", axis=4, tiled=True)
    other = lax.ppermute(tensor, "var", [(0, 1), (1, 0)])
    sums = functools.partial(
        pair_sums, line=line, ids=ids, tables=tables, tensors=(tensor, other)
    )
    for f in range(FREQS):
        if line:
            pairs, inner, outer, inner_far, outer_far = steps[f]
            acc = sums(0, 3, False, freq=f, sources=(spectra[f], pairs, inner, outer))
            keep, send = sums(
                3, 4, True, freq=f, sources=(inner_far, outer_far), acc=acc
            )
        else:
            parts = [whole[f, ..., 128 * b : 128 * (b + 1)] for b in range(SUB_BLOCKS)]
            keep, send = sums(0, 4, True, freq=f, sources=parts)
        kept.append(keep)
        sent.append(send)
    if swap:
        got = [lax.ppermute(send, "sub", [(0, 1), (1, 0)]) for send in sent]
        sums = [keep + more for keep, more in zip(kept, got)]
    else:
        sums = [
            lax.psum_scatter(
                jnp.concatenate(both, axis=2), "sub", scatter_dimension=2, tiled=True
            )
            for both in zip(kept, sent)
        ]
    freq_index = (offset[0] + jnp.arange(FREQS, dtype=jnp.int32)).astype(jnp.float32)
    brune = 1.0 / (1.0 + (freq_index / CORNER) ** 2)
    result = jnp.stack([sums[f] * brune[f] for f in range(FREQS)])
    return result.transpose(0, 1, 2, 4, 3)


def solution(mesh):
    return jax.shard_map(
        functools.partial(shards, mesh.shape["site"], mesh.shape["sub"]),
        mesh=mesh,
        in_specs=(
            P(("scen", "site"), "sub", None, "var", None, None, None, None, None),
            P(None, None, ("scen", "var"), None, ("sub", "site")),
            P(("scen", "site"), "sub", None),
            P(("scen", "site"), "sub", None),
            P(("scen", "site"), "sub", None),
            P("scen"),
        ),
        out_specs=P(None, None, None, "var", ("scen", "site", "sub")),
        check_vma=False,
    )
```

```python
import functools

import jax
import jax.numpy as jnp
from jax import lax
from jax.experimental import pallas as pl
from jax.experimental.pallas import tpu as pltpu
from jax.sharding import PartitionSpec as P

FREQS = 2
SITE_BLOCKS = 4
SUB_BLOCKS = 4
CORNER = 48.0
VMEM_LIMIT = 40 << 20
PREPARE_LIMIT = 50 << 20

SMEM_SPEC = pl.BlockSpec(memory_space=pltpu.SMEM)
VMEM_SPEC = pl.BlockSpec(memory_space=pltpu.VMEM)
HBM_SPEC = pl.BlockSpec(memory_space=pl.ANY)


def place_of(block, z):
    flip = z >= 2
    block = jnp.where(flip, 3 - block, block)
    z = jnp.where(flip, 3 - z, z)
    return jnp.where(block < 2, block ^ z, block)


def prepare_kernel(line, table, own, other, dense, tiles, slot_of, counts, sem):
    z, j, v = table[3, 0], table[3, 1], table[3, 2]
    slots = own.shape[0]
    half = SITE_BLOCKS // 2
    _, _, comps, moments, block_sites, columns = own.shape

    def clear(i, _):
        slot_of[i] = 0
        counts[i] = 0
        return 0

    lax.fori_loop(0, SUB_BLOCKS * SITE_BLOCKS, clear, 0)

    def load(p, _):
        @pl.when(table[2, p] > 0)
        def _():
            pltpu.make_async_copy(own.at[p], tiles.at[0, p], sem).start()
            pltpu.make_async_copy(other.at[p], tiles.at[1, p], sem).start()
            block = table[1, p]
            place = place_of(block, z) if line else block
            s = table[0, p]
            at = place * SITE_BLOCKS + (s // half ^ j) * half + s % half
            slot_of[at] = p
            counts[at] = table[2, p]

        return 0

    lax.fori_loop(0, slots, load, 0)

    def drain(p, _):
        @pl.when(table[2, p] > 0)
        def _():
            pltpu.make_async_copy(own.at[p], tiles.at[0, p], sem).wait()
            pltpu.make_async_copy(other.at[p], tiles.at[1, p], sem).wait()

        return 0

    lax.fori_loop(0, slots, drain, 0)
    lane = lax.broadcasted_iota(jnp.int32, (block_sites, columns), 1)

    def lay(i, _):
        place = i // SITE_BLOCKS
        row = i % SITE_BLOCKS
        slot = slot_of[i]
        live = lane < counts[i]
        for role in range(2):
            f = v if role == 0 else 1 - v
            for r in range(2):
                start = pl.multiple_of((r * SITE_BLOCKS + row) * block_sites, block_sites)
                for c in range(comps):
                    for m in range(moments):
                        value = jnp.where(
                            live, tiles[role, slot, r, c, m], jnp.zeros((), dense.dtype)
                        )
                        dense[
                            f,
                            place,
                            c,
                            pl.ds(start, block_sites),
                            columns * m : columns * (m + 1),
                        ] = value
        return 0

    lax.fori_loop(0, SUB_BLOCKS * SITE_BLOCKS, lay, 0)


def prepare(line, table, own, other):
    slots, _, comps, moments, block_sites, columns = own.shape
    return pl.pallas_call(
        functools.partial(prepare_kernel, line),
        out_shape=pltpu.VMEM(
            (
                FREQS,
                SUB_BLOCKS,
                comps,
                2 * SITE_BLOCKS * block_sites,
                moments * columns,
            ),
            own.dtype,
        ),
        in_specs=[SMEM_SPEC] + [HBM_SPEC] * 2,
        out_specs=VMEM_SPEC,
        scratch_shapes=[
            pltpu.VMEM((2,) + own.shape, own.dtype),
            pltpu.SMEM((SUB_BLOCKS * SITE_BLOCKS,), jnp.int32),
            pltpu.SMEM((SUB_BLOCKS * SITE_BLOCKS,), jnp.int32),
            pltpu.SemaphoreType.DMA,
        ],
        compiler_params=pltpu.CompilerParams(vmem_limit_bytes=PREPARE_LIMIT),
        cost_estimate=pl.CostEstimate(
            flops=0, bytes_accessed=12_000_000, transcendentals=0
        ),
    )(table, own, other)


def products(dense, f, place, c, spectrum):
    moments, variants, columns = spectrum.shape[1:]
    rhs = jnp.concatenate(
        [spectrum[:, m].reshape(2 * variants, columns) for m in range(moments)], axis=1
    )
    total = lax.dot_general(
        dense[f, place, c],
        rhs,
        (((1,), (1,)), ((), ())),
        preferred_element_type=jnp.float32,
    )
    rows = total.shape[0] // 2
    real = total[:rows, :variants] - total[rows:, variants:]
    imag = total[:rows, variants:] + total[rows:, :variants]
    return real, imag


def early_kernel(dense, own, pairs, acc, spec, sem):
    copies = [
        pltpu.make_async_copy(source, spec.at[n], sem.at[n])
        for n, source in enumerate((own, pairs))
    ]
    for copy in copies:
        copy.start()
    for place in range(2):
        copies[place].wait()
        for f in range(FREQS):
            for c in range(dense.shape[2]):
                for r, value in enumerate(products(dense, f, place, c, spec[place, f])):
                    if place == 0:
                        acc[f, r, c] = value
                    else:
                        acc[f, r, c] += value


def early(dense, own, pairs):
    _, _, comps, rows, depth = dense.shape
    variants = own.shape[3]
    return pl.pallas_call(
        early_kernel,
        out_shape=pltpu.VMEM((FREQS, 2, comps, rows // 2, variants), jnp.float32),
        in_specs=[VMEM_SPEC, HBM_SPEC, HBM_SPEC],
        out_specs=VMEM_SPEC,
        scratch_shapes=[
            pltpu.VMEM((2,) + own.shape, own.dtype),
            pltpu.SemaphoreType.DMA((2,)),
        ],
        compiler_params=pltpu.CompilerParams(vmem_limit_bytes=VMEM_LIMIT),
        cost_estimate=pl.CostEstimate(
            flops=8 * comps * rows * 2 * variants * depth,
            bytes_accessed=4_000_000,
            transcendentals=0,
        ),
    )(dense, own, pairs)


def place_sums(dense, f, place, c, spectrum, sums):
    pair = products(dense, f, place, c, spectrum)
    return pair if sums is None else [a + b for a, b in zip(sums, pair)]


def split_halves(sums, c, keep, send):
    half = keep.shape[2]
    for r, value in enumerate(sums):
        keep[r, c] = value[:half]
        send[r, c] = value[half:]


def late_kernel(f, table, dense, acc, *refs):
    places = 2 - f
    sources = refs[: 2 * places]
    *outs, spec, sem = refs[2 * places :]
    is_mid = jnp.logical_and(table[3, 0] > 0, table[3, 0] < 3)

    @pl.when(is_mid)
    def _():
        for n, source in enumerate(sources[:places]):
            pltpu.make_async_copy(source, spec.at[n], sem.at[n]).start()

    @pl.when(jnp.logical_not(is_mid))
    def _():
        for n, source in enumerate(sources[places:]):
            pltpu.make_async_copy(source, spec.at[n], sem.at[n]).start()

    for n in range(places):
        pltpu.make_async_copy(sources[n], spec.at[n], sem.at[n]).wait()
    for c in range(dense.shape[2]):
        sums = [acc[f, r, c] for r in range(2)]
        for n in range(places):
            sums = place_sums(dense, f, 2 + n, c, spec[n], sums)
        if f == 0:
            split_halves(sums, c, *outs)
        else:
            for r, value in enumerate(sums):
                outs[0][r, c] = value


def late(f, table, dense, acc, sources):
    _, _, comps, rows, depth = dense.shape
    shape = sources[0].shape
    places = len(sources) // 2
    half = pltpu.VMEM((2, comps, rows // 4, shape[2]), jnp.float32)
    full = pltpu.VMEM((2, comps, rows // 2, shape[2]), jnp.float32)
    return pl.pallas_call(
        functools.partial(late_kernel, f),
        out_shape=(half, half) if f == 0 else full,
        in_specs=[SMEM_SPEC, VMEM_SPEC, VMEM_SPEC] + [HBM_SPEC] * len(sources),
        out_specs=(VMEM_SPEC, VMEM_SPEC) if f == 0 else VMEM_SPEC,
        scratch_shapes=[
            pltpu.VMEM((places,) + shape, dense.dtype),
            pltpu.SemaphoreType.DMA((places,)),
        ],
        compiler_params=pltpu.CompilerParams(vmem_limit_bytes=VMEM_LIMIT),
        cost_estimate=pl.CostEstimate(
            flops=2 * places * comps * rows * 2 * shape[2] * depth,
            bytes_accessed=800_000 * places,
            transcendentals=0,
        ),
    )(table, dense, acc, *sources)


def last_kernel(table, dense, acc, middle, far, keep, send):
    is_mid = jnp.logical_and(table[3, 0] > 0, table[3, 0] < 3)

    def run(source):
        for c in range(dense.shape[2]):
            sums = [acc[r, c] for r in range(2)]
            split_halves(place_sums(dense, 1, 3, c, source[...], sums), c, keep, send)

    @pl.when(is_mid)
    def _():
        run(middle)

    @pl.when(jnp.logical_not(is_mid))
    def _():
        run(far)


def last(table, dense, acc, middle, far):
    _, _, comps, rows, depth = dense.shape
    half = (2, comps, rows // 4, middle.shape[2])
    return pl.pallas_call(
        last_kernel,
        out_shape=(pltpu.VMEM(half, jnp.float32),) * 2,
        in_specs=[SMEM_SPEC] + [VMEM_SPEC] * 4,
        out_specs=(VMEM_SPEC,) * 2,
        compiler_params=pltpu.CompilerParams(vmem_limit_bytes=VMEM_LIMIT),
        cost_estimate=pl.CostEstimate(
            flops=2 * comps * rows * 2 * middle.shape[2] * depth,
            bytes_accessed=1_000_000,
            transcendentals=0,
        ),
    )(table, dense, acc, middle, far)


def whole_kernel(f, dense, parts, keep, send, spec, sem):
    copy = pltpu.make_async_copy(parts, spec, sem)
    copy.start()
    copy.wait()
    for c in range(dense.shape[2]):
        sums = None
        for place in range(SUB_BLOCKS):
            sums = place_sums(dense, f, place, c, spec[place], sums)
        split_halves(sums, c, keep, send)


def whole(f, dense, parts):
    _, _, comps, rows, depth = dense.shape
    half = jax.ShapeDtypeStruct((2, comps, rows // 4, parts.shape[3]), jnp.float32)
    return pl.pallas_call(
        functools.partial(whole_kernel, f),
        out_shape=(half, half),
        in_specs=[VMEM_SPEC, HBM_SPEC],
        out_specs=(VMEM_SPEC,) * 2,
        scratch_shapes=[
            pltpu.VMEM(parts.shape, parts.dtype),
            pltpu.SemaphoreType.DMA,
        ],
        compiler_params=pltpu.CompilerParams(vmem_limit_bytes=VMEM_LIMIT),
    )(dense, parts)


def finish_kernel(brune, *refs):
    result, value, sem = refs[-3:]
    copies = []
    for f in range(FREQS):
        keep, got = refs[2 * f : 2 * f + 2]
        for r in range(2):
            value[f, r] = (keep[r] + got[r]) * brune[f]
            copy = pltpu.make_async_copy(value.at[f, r], result.at[f, r], sem.at[f, r])
            copy.start()
            copies.append(copy)
    for copy in copies:
        copy.wait()


def finish(brune, pieces):
    shape = (FREQS,) + pieces[0].shape
    return pl.pallas_call(
        finish_kernel,
        out_shape=jax.ShapeDtypeStruct(shape, pieces[0].dtype),
        in_specs=[SMEM_SPEC] + [VMEM_SPEC] * len(pieces),
        out_specs=HBM_SPEC,
        scratch_shapes=[
            pltpu.VMEM(shape, pieces[0].dtype),
            pltpu.SemaphoreType.DMA((FREQS, 2)),
        ],
        compiler_params=pltpu.CompilerParams(vmem_limit_bytes=VMEM_LIMIT),
        cost_estimate=pl.CostEstimate(
            flops=400_000, bytes_accessed=600_000, transcendentals=0
        ),
    )(brune, *pieces)


def after(value, *others):
    return lax.optimization_barrier((value, *others))[0]


PAIRS = [(0, 1), (1, 0), (2, 3), (3, 2)]
INNER = [(1, 2), (2, 1)]
OUTER = [(1, 0), (2, 3)]


def line_steps(own, dense):
    move = functools.partial(lax.ppermute, axis_name="site")
    pairs = move(own, perm=PAIRS)
    inner = [move(own[f], perm=INNER) for f in range(FREQS)]
    outer = [move(inner[f], perm=OUTER) for f in range(FREQS)]
    ready = after(pairs, dense)
    middle = [move(after(ready[f], *inner), perm=INNER) for f in range(FREQS)]
    acc = early(dense, own, pairs)
    far = [move(after(middle[f], outer[f], acc), perm=OUTER) for f in range(FREQS)]
    first, second = zip(inner, middle, outer, far)
    return acc, first, second


def exchange(send):
    return lax.ppermute(send, "sub", [(0, 1), (1, 0)])


def shards(n_site, n_sub, tensor, spectra, pair_site, pair_block, pair_count, offset):
    spectra = spectra.transpose(0, 1, 3, 2, 4)
    tensor = tensor[0, 0, :, 0].transpose(0, 1, 2, 4, 3, 5)
    swap = n_sub == 2
    line = swap and n_site == SUB_BLOCKS
    half = lax.axis_index("sub") if swap else 0
    ids = jnp.stack([lax.axis_index("site"), half, lax.axis_index("var")])
    ids = jnp.pad(ids.astype(jnp.int32), (0, tensor.shape[0] - 3))
    table = jnp.stack([pair_site[0, 0], pair_block[0, 0], pair_count[0, 0], ids])
    freq_index = (offset[0] + jnp.arange(FREQS, dtype=jnp.int32)).astype(jnp.float32)
    brune = 1.0 / (1.0 + (freq_index / CORNER) ** 2)
    other = lax.ppermute(tensor, "var", [(0, 1), (1, 0)])
    dense = prepare(line, table, tensor, other)
    if line:
        acc, first, second = line_steps(spectra, dense)
        inner1, middle1, outer1, far1 = second
        keep, send = late(0, table, dense, acc, first)
        pieces = [keep, exchange(send)]
        more = late(1, table, dense, acc, (inner1, outer1))
        far1 = after(far1, pieces[1], more)
        keep, send = last(table, dense, more, middle1, far1)
        pieces += [keep, exchange(send)]
    else:
        gathered = lax.all_gather(spectra, "site", axis=4, tiled=True)
        pieces = []
        for f in range(FREQS):
            blocks = gathered[f].reshape(gathered.shape[1:4] + (SUB_BLOCKS, -1))
            keep, send = whole(f, dense, blocks.transpose(3, 0, 1, 2, 4))
            if swap:
                pieces += [keep, exchange(send)]
            else:
                both = jnp.concatenate([keep, send], axis=2)
                keep = lax.psum_scatter(both, "sub", scatter_dimension=2, tiled=True)
                pieces += [keep, jnp.zeros_like(keep)]
    result = finish(brune, pieces)
    return result.transpose(0, 1, 2, 4, 3)


def solution(mesh):
    return jax.shard_map(
        functools.partial(shards, mesh.shape["site"], mesh.shape["sub"]),
        mesh=mesh,
        in_specs=(
            P(("scen", "site"), "sub", None, "var", None, None, None, None, None),
            P(None, None, ("scen", "var"), None, ("sub", "site")),
            P(("scen", "site"), "sub", None),
            P(("scen", "site"), "sub", None),
            P(("scen", "site"), "sub", None),
            P("scen"),
        ),
        out_specs=P(None, None, None, "var", ("scen", "site", "sub")),
        check_vma=False,
    )
```

```python
import functools

import jax
import jax.numpy as jnp
from jax import lax
from jax.experimental import pallas as pl
from jax.experimental.pallas import tpu as pltpu
from jax.sharding import PartitionSpec as P

FREQS = 2
SITE_BLOCKS = 4
SUB_BLOCKS = 4
CORNER = 48.0
VMEM_LIMIT = 40 << 20
PREPARE_LIMIT = 50 << 20

SMEM_SPEC = pl.BlockSpec(memory_space=pltpu.SMEM)
VMEM_SPEC = pl.BlockSpec(memory_space=pltpu.VMEM)
HBM_SPEC = pl.BlockSpec(memory_space=pl.ANY)


def place_of(block, z):
    flip = z >= 2
    block = jnp.where(flip, 3 - block, block)
    z = jnp.where(flip, 3 - z, z)
    return jnp.where(block < 2, block ^ z, block)


def prepare_kernel(line, table, own, other, dense, tiles, slot_of, counts, sem):
    z, j, v = table[3, 0], table[3, 1], table[3, 2]
    slots = own.shape[0]
    half = SITE_BLOCKS // 2
    _, _, comps, moments, block_sites, columns = own.shape

    def clear(i, _):
        slot_of[i] = 0
        counts[i] = 0
        return 0

    lax.fori_loop(0, SUB_BLOCKS * SITE_BLOCKS, clear, 0)

    def load(p, _):
        @pl.when(table[2, p] > 0)
        def _():
            pltpu.make_async_copy(own.at[p], tiles.at[0, p], sem).start()
            pltpu.make_async_copy(other.at[p], tiles.at[1, p], sem).start()
            block = table[1, p]
            place = place_of(block, z) if line else block
            s = table[0, p]
            at = place * SITE_BLOCKS + (s // half ^ j) * half + s % half
            slot_of[at] = p
            counts[at] = table[2, p]

        return 0

    lax.fori_loop(0, slots, load, 0)

    def drain(p, _):
        @pl.when(table[2, p] > 0)
        def _():
            pltpu.make_async_copy(own.at[p], tiles.at[0, p], sem).wait()
            pltpu.make_async_copy(other.at[p], tiles.at[1, p], sem).wait()

        return 0

    lax.fori_loop(0, slots, drain, 0)
    lane = lax.broadcasted_iota(jnp.int32, (block_sites, columns), 1)

    def lay(i, _):
        place = i // SITE_BLOCKS
        row = i % SITE_BLOCKS
        slot = slot_of[i]
        live = lane < counts[i]
        for role in range(2):
            f = v if role == 0 else 1 - v
            for r in range(2):
                start = pl.multiple_of((r * SITE_BLOCKS + row) * block_sites, block_sites)
                for c in range(comps):
                    for m in range(moments):
                        value = jnp.where(
                            live, tiles[role, slot, r, c, m], jnp.zeros((), dense.dtype)
                        )
                        dense[
                            f,
                            place,
                            c,
                            pl.ds(start, block_sites),
                            columns * m : columns * (m + 1),
                        ] = value
        return 0

    lax.fori_loop(0, SUB_BLOCKS * SITE_BLOCKS, lay, 0)


def prepare(line, table, own, other):
    slots, _, comps, moments, block_sites, columns = own.shape
    return pl.pallas_call(
        functools.partial(prepare_kernel, line),
        out_shape=pltpu.VMEM(
            (
                FREQS,
                SUB_BLOCKS,
                comps,
                2 * SITE_BLOCKS * block_sites,
                moments * columns,
            ),
            own.dtype,
        ),
        in_specs=[SMEM_SPEC] + [HBM_SPEC] * 2,
        out_specs=VMEM_SPEC,
        scratch_shapes=[
            pltpu.VMEM((2,) + own.shape, own.dtype),
            pltpu.SMEM((SUB_BLOCKS * SITE_BLOCKS,), jnp.int32),
            pltpu.SMEM((SUB_BLOCKS * SITE_BLOCKS,), jnp.int32),
            pltpu.SemaphoreType.DMA,
        ],
        compiler_params=pltpu.CompilerParams(vmem_limit_bytes=PREPARE_LIMIT),
        cost_estimate=pl.CostEstimate(
            flops=0, bytes_accessed=12_000_000, transcendentals=0
        ),
    )(table, own, other)


def products(dense, f, place, c, spectrum):
    moments, variants, columns = spectrum.shape[1:]
    rhs = jnp.concatenate(
        [spectrum[:, m].reshape(2 * variants, columns) for m in range(moments)], axis=1
    )
    total = lax.dot_general(
        dense[f, place, c],
        rhs,
        (((1,), (1,)), ((), ())),
        preferred_element_type=jnp.float32,
    )
    rows = total.shape[0] // 2
    real = total[:rows, :variants] - total[rows:, variants:]
    imag = total[:rows, variants:] + total[rows:, :variants]
    return real, imag


def early_kernel(dense, own, pairs, acc, spec, sem):
    copies = [
        pltpu.make_async_copy(source, spec.at[n], sem.at[n])
        for n, source in enumerate((own, pairs))
    ]
    for copy in copies:
        copy.start()
    for place in range(2):
        copies[place].wait()
        for f in range(FREQS):
            for c in range(dense.shape[2]):
                for r, value in enumerate(products(dense, f, place, c, spec[place, f])):
                    if place == 0:
                        acc[f, r, c] = value
                    else:
                        acc[f, r, c] += value


def early(dense, own, pairs):
    _, _, comps, rows, depth = dense.shape
    variants = own.shape[3]
    return pl.pallas_call(
        early_kernel,
        out_shape=pltpu.VMEM((FREQS, 2, comps, rows // 2, variants), jnp.float32),
        in_specs=[VMEM_SPEC, HBM_SPEC, HBM_SPEC],
        out_specs=VMEM_SPEC,
        scratch_shapes=[
            pltpu.VMEM((2,) + own.shape, own.dtype),
            pltpu.SemaphoreType.DMA((2,)),
        ],
        compiler_params=pltpu.CompilerParams(vmem_limit_bytes=VMEM_LIMIT),
        cost_estimate=pl.CostEstimate(
            flops=8 * comps * rows * 2 * variants * depth,
            bytes_accessed=4_000_000,
            transcendentals=0,
        ),
    )(dense, own, pairs)


def place_sums(dense, f, place, c, spectrum, sums):
    pair = products(dense, f, place, c, spectrum)
    return pair if sums is None else [a + b for a, b in zip(sums, pair)]


def split_halves(sums, c, keep, send):
    half = keep.shape[2]
    for r, value in enumerate(sums):
        keep[r, c] = value[:half]
        send[r, c] = value[half:]


def late_kernel(f, table, dense, acc, *refs):
    places = 2 - f
    sources = refs[: 2 * places]
    *outs, spec, sem = refs[2 * places :]
    is_mid = jnp.logical_and(table[3, 0] > 0, table[3, 0] < 3)

    @pl.when(is_mid)
    def _():
        for n, source in enumerate(sources[:places]):
            pltpu.make_async_copy(source, spec.at[n], sem.at[n]).start()

    @pl.when(jnp.logical_not(is_mid))
    def _():
        for n, source in enumerate(sources[places:]):
            pltpu.make_async_copy(source, spec.at[n], sem.at[n]).start()

    for n in range(places):
        pltpu.make_async_copy(sources[n], spec.at[n], sem.at[n]).wait()
    for c in range(dense.shape[2]):
        sums = [acc[f, r, c] for r in range(2)]
        for n in range(places):
            sums = place_sums(dense, f, 2 + n, c, spec[n], sums)
        if f == 0:
            split_halves(sums, c, *outs)
        else:
            for r, value in enumerate(sums):
                outs[0][r, c] = value


def late(f, table, dense, acc, sources):
    _, _, comps, rows, depth = dense.shape
    shape = sources[0].shape
    places = len(sources) // 2
    half = pltpu.VMEM((2, comps, rows // 4, shape[2]), jnp.float32)
    full = pltpu.VMEM((2, comps, rows // 2, shape[2]), jnp.float32)
    return pl.pallas_call(
        functools.partial(late_kernel, f),
        out_shape=(half, half) if f == 0 else full,
        in_specs=[SMEM_SPEC, VMEM_SPEC, VMEM_SPEC] + [HBM_SPEC] * len(sources),
        out_specs=(VMEM_SPEC, VMEM_SPEC) if f == 0 else VMEM_SPEC,
        scratch_shapes=[
            pltpu.VMEM((places,) + shape, dense.dtype),
            pltpu.SemaphoreType.DMA((places,)),
        ],
        compiler_params=pltpu.CompilerParams(vmem_limit_bytes=VMEM_LIMIT),
        cost_estimate=pl.CostEstimate(
            flops=2 * places * comps * rows * 2 * shape[2] * depth,
            bytes_accessed=800_000 * places,
            transcendentals=0,
        ),
    )(table, dense, acc, *sources)


def last_kernel(dense, acc, middle, far, keep, send):
    z = lax.axis_index("site")
    is_mid = jnp.logical_and(z > 0, z < 3)

    def run(source):
        for c in range(dense.shape[2]):
            sums = [acc[r, c] for r in range(2)]
            split_halves(place_sums(dense, 1, 3, c, source[...], sums), c, keep, send)

    @pl.when(is_mid)
    def _():
        run(middle)

    @pl.when(jnp.logical_not(is_mid))
    def _():
        run(far)


def last(dense, acc, middle, far):
    _, _, comps, rows, depth = dense.shape
    half = (2, comps, rows // 4, middle.shape[2])
    return pl.pallas_call(
        last_kernel,
        out_shape=(pltpu.VMEM(half, jnp.float32),) * 2,
        in_specs=[VMEM_SPEC] * 4,
        out_specs=(VMEM_SPEC,) * 2,
        compiler_params=pltpu.CompilerParams(vmem_limit_bytes=VMEM_LIMIT),
        cost_estimate=pl.CostEstimate(
            flops=2 * comps * rows * 2 * middle.shape[2] * depth,
            bytes_accessed=1_000_000,
            transcendentals=0,
        ),
    )(dense, acc, middle, far)


def whole_kernel(f, dense, parts, keep, send, spec, sem):
    copy = pltpu.make_async_copy(parts, spec, sem)
    copy.start()
    copy.wait()
    for c in range(dense.shape[2]):
        sums = None
        for place in range(SUB_BLOCKS):
            sums = place_sums(dense, f, place, c, spec[place], sums)
        split_halves(sums, c, keep, send)


def whole(f, dense, parts):
    _, _, comps, rows, depth = dense.shape
    half = jax.ShapeDtypeStruct((2, comps, rows // 4, parts.shape[3]), jnp.float32)
    return pl.pallas_call(
        functools.partial(whole_kernel, f),
        out_shape=(half, half),
        in_specs=[VMEM_SPEC, HBM_SPEC],
        out_specs=(VMEM_SPEC,) * 2,
        scratch_shapes=[
            pltpu.VMEM(parts.shape, parts.dtype),
            pltpu.SemaphoreType.DMA,
        ],
        compiler_params=pltpu.CompilerParams(vmem_limit_bytes=VMEM_LIMIT),
    )(dense, parts)


def finish_kernel(brune, *refs):
    result, value, sem = refs[-3:]
    copies = []
    for f in range(FREQS):
        keep, got = refs[2 * f : 2 * f + 2]
        for r in range(2):
            value[f, r] = (keep[r] + got[r]) * brune[f, :1]
            copy = pltpu.make_async_copy(value.at[f, r], result.at[f, r], sem.at[f, r])
            copy.start()
            copies.append(copy)
    for copy in copies:
        copy.wait()


def finish(brune, pieces):
    shape = (FREQS,) + pieces[0].shape
    return pl.pallas_call(
        finish_kernel,
        out_shape=jax.ShapeDtypeStruct(shape, pieces[0].dtype),
        in_specs=[VMEM_SPEC] * (1 + len(pieces)),
        out_specs=HBM_SPEC,
        scratch_shapes=[
            pltpu.VMEM(shape, pieces[0].dtype),
            pltpu.SemaphoreType.DMA((FREQS, 2)),
        ],
        compiler_params=pltpu.CompilerParams(vmem_limit_bytes=VMEM_LIMIT),
        cost_estimate=pl.CostEstimate(
            flops=400_000, bytes_accessed=600_000, transcendentals=0
        ),
    )(brune, *pieces)


def after(value, *others):
    return lax.optimization_barrier((value, *others))[0]


PAIRS = [(0, 1), (1, 0), (2, 3), (3, 2)]
INNER = [(1, 2), (2, 1)]
OUTER = [(1, 0), (2, 3)]


def line_steps(own, dense):
    move = functools.partial(lax.ppermute, axis_name="site")
    pairs = move(own, perm=PAIRS)
    inner = [move(own[f], perm=INNER) for f in range(FREQS)]
    outer = [move(inner[f], perm=OUTER) for f in range(FREQS)]
    ready = after(pairs, dense)
    acc = early(dense, own, pairs)
    middle = [move(after(ready[0], inner[0]), perm=INNER), move(after(ready[1], *inner, acc), perm=INNER)]
    far = [move(after(middle[f], outer[f], acc), perm=OUTER) for f in range(FREQS)]
    first, second = zip(inner, middle, outer, far)
    return acc, first, second


def exchange(send):
    return lax.ppermute(send, "sub", [(0, 1), (1, 0)])


def shards(n_site, n_sub, tensor, spectra, pair_site, pair_block, pair_count, offset):
    spectra = spectra.transpose(0, 1, 3, 2, 4)
    tensor = tensor[0, 0, :, 0].transpose(0, 1, 2, 4, 3, 5)
    swap = n_sub == 2
    line = swap and n_site == SUB_BLOCKS
    half = lax.axis_index("sub") if swap else 0
    ids = jnp.stack([lax.axis_index("site"), half, lax.axis_index("var")])
    ids = jnp.pad(ids.astype(jnp.int32), (0, tensor.shape[0] - 3))
    table = jnp.stack([pair_site[0, 0], pair_block[0, 0], pair_count[0, 0], ids])
    freq_index = (offset[0] + jnp.arange(FREQS, dtype=jnp.int32)).astype(jnp.float32)
    brune = 1.0 / (1.0 + (freq_index / CORNER) ** 2)
    other = lax.ppermute(tensor, "var", [(0, 1), (1, 0)])
    dense = prepare(line, table, tensor, other)
    if line:
        acc, first, second = line_steps(spectra, dense)
        inner1, middle1, outer1, far1 = second
        keep, send = late(0, table, dense, acc, first)
        pieces = [keep, exchange(send)]
        more = late(1, table, dense, acc, (inner1, outer1))
        far1 = after(far1, pieces[1], more)
        keep, send = last(dense, more, middle1, far1)
        pieces += [keep, exchange(send)]
    else:
        gathered = lax.all_gather(spectra, "site", axis=4, tiled=True)
        pieces = []
        for f in range(FREQS):
            blocks = gathered[f].reshape(gathered.shape[1:4] + (SUB_BLOCKS, -1))
            keep, send = whole(f, dense, blocks.transpose(3, 0, 1, 2, 4))
            if swap:
                pieces += [keep, exchange(send)]
            else:
                both = jnp.concatenate([keep, send], axis=2)
                keep = lax.psum_scatter(both, "sub", scatter_dimension=2, tiled=True)
                pieces += [keep, jnp.zeros_like(keep)]
    rows = jnp.broadcast_to(brune[:, None, None], (FREQS, 8, pieces[0].shape[3]))
    result = finish(rows, pieces)
    return result.transpose(0, 1, 2, 4, 3)


def solution(mesh):
    return jax.shard_map(
        functools.partial(shards, mesh.shape["site"], mesh.shape["sub"]),
        mesh=mesh,
        in_specs=(
            P(("scen", "site"), "sub", None, "var", None, None, None, None, None),
            P(None, None, ("scen", "var"), None, ("sub", "site")),
            P(("scen", "site"), "sub", None),
            P(("scen", "site"), "sub", None),
            P(("scen", "site"), "sub", None),
            P("scen"),
        ),
        out_specs=P(None, None, None, "var", ("scen", "site", "sub")),
        check_vma=False,
    )
```

```python
import functools

import jax
import jax.numpy as jnp
from jax import lax
from jax.experimental import pallas as pl
from jax.experimental.pallas import tpu as pltpu
from jax.sharding import PartitionSpec as P

FREQS = 2
SITE_BLOCKS = 4
SUB_BLOCKS = 4
CORNER = 48.0
VMEM_LIMIT = 40 << 20
PREPARE_LIMIT = 50 << 20

SMEM_SPEC = pl.BlockSpec(memory_space=pltpu.SMEM)
VMEM_SPEC = pl.BlockSpec(memory_space=pltpu.VMEM)
HBM_SPEC = pl.BlockSpec(memory_space=pl.ANY)


def place_of(block, z):
    flip = z >= 2
    block = jnp.where(flip, 3 - block, block)
    z = jnp.where(flip, 3 - z, z)
    return jnp.where(block < 2, block ^ z, block)


def prepare_kernel(line, table, own, other, dense, tiles, slot_of, counts, sem):
    z, j, v = table[3, 0], table[3, 1], table[3, 2]
    slots = own.shape[0]
    half = SITE_BLOCKS // 2
    _, _, comps, moments, block_sites, columns = own.shape

    def clear(i, _):
        slot_of[i] = 0
        counts[i] = 0
        return 0

    lax.fori_loop(0, SUB_BLOCKS * SITE_BLOCKS, clear, 0)

    def load(p, _):
        @pl.when(table[2, p] > 0)
        def _():
            pltpu.make_async_copy(own.at[p], tiles.at[0, p], sem).start()
            pltpu.make_async_copy(other.at[p], tiles.at[1, p], sem).start()
            block = table[1, p]
            place = place_of(block, z) if line else block
            s = table[0, p]
            at = place * SITE_BLOCKS + (s // half ^ j) * half + s % half
            slot_of[at] = p
            counts[at] = table[2, p]

        return 0

    lax.fori_loop(0, slots, load, 0)

    def drain(p, _):
        @pl.when(table[2, p] > 0)
        def _():
            pltpu.make_async_copy(own.at[p], tiles.at[0, p], sem).wait()
            pltpu.make_async_copy(other.at[p], tiles.at[1, p], sem).wait()

        return 0

    lax.fori_loop(0, slots, drain, 0)
    lane = lax.broadcasted_iota(jnp.int32, (block_sites, columns), 1)

    def lay(i, _):
        place = i // SITE_BLOCKS
        row = i % SITE_BLOCKS
        slot = slot_of[i]
        live = lane < counts[i]
        for role in range(2):
            f = v if role == 0 else 1 - v
            for r in range(2):
                start = pl.multiple_of((r * SITE_BLOCKS + row) * block_sites, block_sites)
                for c in range(comps):
                    for m in range(moments):
                        value = jnp.where(
                            live, tiles[role, slot, r, c, m], jnp.zeros((), dense.dtype)
                        )
                        dense[
                            f,
                            place,
                            c,
                            pl.ds(start, block_sites),
                            columns * m : columns * (m + 1),
                        ] = value
        return 0

    lax.fori_loop(0, SUB_BLOCKS * SITE_BLOCKS, lay, 0)


def prepare(line, table, own, other):
    slots, _, comps, moments, block_sites, columns = own.shape
    return pl.pallas_call(
        functools.partial(prepare_kernel, line),
        out_shape=pltpu.VMEM(
            (
                FREQS,
                SUB_BLOCKS,
                comps,
                2 * SITE_BLOCKS * block_sites,
                moments * columns,
            ),
            own.dtype,
        ),
        in_specs=[SMEM_SPEC] + [HBM_SPEC] * 2,
        out_specs=VMEM_SPEC,
        scratch_shapes=[
            pltpu.VMEM((2,) + own.shape, own.dtype),
            pltpu.SMEM((SUB_BLOCKS * SITE_BLOCKS,), jnp.int32),
            pltpu.SMEM((SUB_BLOCKS * SITE_BLOCKS,), jnp.int32),
            pltpu.SemaphoreType.DMA,
        ],
        compiler_params=pltpu.CompilerParams(vmem_limit_bytes=PREPARE_LIMIT),
        cost_estimate=pl.CostEstimate(
            flops=0, bytes_accessed=12_000_000, transcendentals=0
        ),
    )(table, own, other)


def products(dense, f, place, c, spectrum):
    moments, variants, columns = spectrum.shape[1:]
    rhs = jnp.concatenate(
        [spectrum[:, m].reshape(2 * variants, columns) for m in range(moments)], axis=1
    )
    total = lax.dot_general(
        dense[f, place, c],
        rhs,
        (((1,), (1,)), ((), ())),
        preferred_element_type=jnp.float32,
    )
    rows = total.shape[0] // 2
    real = total[:rows, :variants] - total[rows:, variants:]
    imag = total[:rows, variants:] + total[rows:, :variants]
    return real, imag


def early_kernel(dense, own, pairs, acc, spec, sem):
    copies = [
        pltpu.make_async_copy(source, spec.at[n], sem.at[n])
        for n, source in enumerate((own, pairs))
    ]
    for copy in copies:
        copy.start()
    for place in range(2):
        copies[place].wait()
        for f in range(FREQS):
            for c in range(dense.shape[2]):
                for r, value in enumerate(products(dense, f, place, c, spec[place, f])):
                    if place == 0:
                        acc[f, r, c] = value
                    else:
                        acc[f, r, c] += value


def early(dense, own, pairs):
    _, _, comps, rows, depth = dense.shape
    variants = own.shape[3]
    return pl.pallas_call(
        early_kernel,
        out_shape=pltpu.VMEM((FREQS, 2, comps, rows // 2, variants), jnp.float32),
        in_specs=[VMEM_SPEC, HBM_SPEC, HBM_SPEC],
        out_specs=VMEM_SPEC,
        scratch_shapes=[
            pltpu.VMEM((2,) + own.shape, own.dtype),
            pltpu.SemaphoreType.DMA((2,)),
        ],
        compiler_params=pltpu.CompilerParams(vmem_limit_bytes=VMEM_LIMIT),
        cost_estimate=pl.CostEstimate(
            flops=8 * comps * rows * 2 * variants * depth,
            bytes_accessed=4_000_000,
            transcendentals=0,
        ),
    )(dense, own, pairs)


def place_sums(dense, f, place, c, spectrum, sums):
    pair = products(dense, f, place, c, spectrum)
    return pair if sums is None else [a + b for a, b in zip(sums, pair)]


def swap_lanes(value):
    return pltpu.roll(value, value.shape[1] // 2, axis=1)


def low_lanes(value):
    lane = lax.broadcasted_iota(jnp.int32, value.shape, 1)
    return lane < value.shape[1] // 2


def repack(first, second):
    low = low_lanes(first)
    return (
        jnp.where(low, first, swap_lanes(second)),
        jnp.where(low, swap_lanes(first), second),
    )


def split_halves(sums, c, keep, send):
    half = keep.shape[2]
    for r, value in enumerate(sums):
        keep[r, c] = value[:half]
        send[r, c] = value[half:]


def by_position(run, middle, end):
    z = lax.axis_index("site")
    is_mid = jnp.logical_and(z > 0, z < 3)

    @pl.when(is_mid)
    def _():
        run(middle)

    @pl.when(jnp.logical_not(is_mid))
    def _():
        run(end)


def third_kernel(f, dense, acc, inner, outer, total):
    def run(source):
        for c in range(dense.shape[2]):
            sums = [acc[f, r, c] for r in range(2)]
            sums = place_sums(dense, f, 2, c, source[...], sums)
            for n, value in enumerate(sums if f == 0 else repack(*sums)):
                total[n, c] = value

    by_position(run, inner, outer)


def third(f, dense, acc, inner, outer):
    _, _, comps, rows, depth = dense.shape
    variants = inner.shape[2]
    return pl.pallas_call(
        functools.partial(third_kernel, f),
        out_shape=pltpu.VMEM((2, comps, rows // 2, variants), jnp.float32),
        in_specs=[VMEM_SPEC] * 4,
        out_specs=VMEM_SPEC,
        compiler_params=pltpu.CompilerParams(vmem_limit_bytes=VMEM_LIMIT),
        cost_estimate=pl.CostEstimate(
            flops=2 * comps * rows * 2 * variants * depth,
            bytes_accessed=1_000_000,
            transcendentals=0,
        ),
    )(dense, acc, inner, outer)


def fourth_kernel(dense, acc, middle, far, keep, send):
    def run(source):
        for c in range(dense.shape[2]):
            sums = [acc[r, c] for r in range(2)]
            split_halves(place_sums(dense, 0, 3, c, source[...], sums), c, keep, send)

    by_position(run, middle, far)


def fourth(dense, acc, middle, far):
    _, _, comps, rows, depth = dense.shape
    half = (2, comps, rows // 4, middle.shape[2])
    return pl.pallas_call(
        fourth_kernel,
        out_shape=(pltpu.VMEM(half, jnp.float32),) * 2,
        in_specs=[VMEM_SPEC] * 4,
        out_specs=(VMEM_SPEC,) * 2,
        compiler_params=pltpu.CompilerParams(vmem_limit_bytes=VMEM_LIMIT),
        cost_estimate=pl.CostEstimate(
            flops=2 * comps * rows * 2 * middle.shape[2] * depth,
            bytes_accessed=1_000_000,
            transcendentals=0,
        ),
    )(dense, acc, middle, far)


def last_kernel(h, dense, acc, middle, far, keep, send):
    moments, width, columns = far.shape[1:]
    half = keep.shape[1]

    def run(source):
        at = h * width if source is middle else 0
        rhs = jnp.concatenate(
            [
                source[:, m, at : at + width].reshape(2 * width, columns)
                for m in range(moments)
            ],
            axis=1,
        )
        for c in range(dense.shape[2]):
            total = lax.dot_general(
                dense[1, 3, c],
                rhs,
                (((1,), (1,)), ((), ())),
                preferred_element_type=jnp.float32,
            )
            crossed = swap_lanes(total[2 * half :])
            crossed = jnp.where(low_lanes(crossed), -crossed, crossed)
            value = acc[h, c] + (total[: 2 * half] + crossed)
            keep[c] = value[:half]
            send[c] = value[half:]

    by_position(run, middle, far)


def last(h, dense, acc, middle, far):
    _, _, comps, rows, depth = dense.shape
    half = (comps, rows // 4, 2 * far.shape[2])
    return pl.pallas_call(
        functools.partial(last_kernel, h),
        out_shape=(pltpu.VMEM(half, jnp.float32),) * 2,
        in_specs=[VMEM_SPEC] * 4,
        out_specs=(VMEM_SPEC,) * 2,
        compiler_params=pltpu.CompilerParams(vmem_limit_bytes=VMEM_LIMIT),
        cost_estimate=pl.CostEstimate(
            flops=2 * comps * rows * half[2] * depth,
            bytes_accessed=500_000,
            transcendentals=0,
        ),
    )(dense, acc, middle, far)


def whole_kernel(f, dense, parts, keep, send, spec, sem):
    copy = pltpu.make_async_copy(parts, spec, sem)
    copy.start()
    copy.wait()
    for c in range(dense.shape[2]):
        sums = None
        for place in range(SUB_BLOCKS):
            sums = place_sums(dense, f, place, c, spec[place], sums)
        split_halves(sums, c, keep, send)


def whole(f, dense, parts):
    _, _, comps, rows, depth = dense.shape
    half = jax.ShapeDtypeStruct((2, comps, rows // 4, parts.shape[3]), jnp.float32)
    return pl.pallas_call(
        functools.partial(whole_kernel, f),
        out_shape=(half, half),
        in_specs=[VMEM_SPEC, HBM_SPEC],
        out_specs=(VMEM_SPEC,) * 2,
        scratch_shapes=[
            pltpu.VMEM(parts.shape, parts.dtype),
            pltpu.SemaphoreType.DMA,
        ],
        compiler_params=pltpu.CompilerParams(vmem_limit_bytes=VMEM_LIMIT),
    )(dense, parts)


def finish_kernel(brune, *refs):
    result, value, sem = refs[-3:]
    copies = []
    for f in range(FREQS):
        keep, got = refs[2 * f : 2 * f + 2]
        for r in range(2):
            value[f, r] = (keep[r] + got[r]) * brune[f, :1]
            copy = pltpu.make_async_copy(value.at[f, r], result.at[f, r], sem.at[f, r])
            copy.start()
            copies.append(copy)
    for copy in copies:
        copy.wait()


def finish(brune, pieces):
    shape = (FREQS,) + pieces[0].shape
    return pl.pallas_call(
        finish_kernel,
        out_shape=jax.ShapeDtypeStruct(shape, pieces[0].dtype),
        in_specs=[VMEM_SPEC] * (1 + len(pieces)),
        out_specs=HBM_SPEC,
        scratch_shapes=[
            pltpu.VMEM(shape, pieces[0].dtype),
            pltpu.SemaphoreType.DMA((FREQS, 2)),
        ],
        compiler_params=pltpu.CompilerParams(vmem_limit_bytes=VMEM_LIMIT),
        cost_estimate=pl.CostEstimate(
            flops=400_000, bytes_accessed=600_000, transcendentals=0
        ),
    )(brune, *pieces)


def finish_first_kernel(brune, keep, got, keep_a, got_a, result, part, value, sem):
    copies = []
    for r in range(2):
        value[r] = (keep[r] + got[r]) * brune[0, :1]
        copies.append(
            pltpu.make_async_copy(value.at[r], result.at[0, r], sem.at[r])
        )
        copies[r].start()
    part[...] = (keep_a[...] + got_a[...]) * brune[1, :1]
    for copy in copies:
        copy.wait()


def finish_first(brune, keep, got, keep_a, got_a):
    return pl.pallas_call(
        finish_first_kernel,
        out_shape=(
            jax.ShapeDtypeStruct((FREQS,) + keep.shape, keep.dtype),
            pltpu.VMEM(keep_a.shape, keep.dtype),
        ),
        in_specs=[VMEM_SPEC] * 5,
        out_specs=(HBM_SPEC, VMEM_SPEC),
        scratch_shapes=[
            pltpu.VMEM(keep.shape, keep.dtype),
            pltpu.SemaphoreType.DMA((2,)),
        ],
        compiler_params=pltpu.CompilerParams(vmem_limit_bytes=VMEM_LIMIT),
        cost_estimate=pl.CostEstimate(
            flops=400_000, bytes_accessed=8_000_000, transcendentals=0
        ),
    )(brune, keep, got, keep_a, got_a)


def finish_last_kernel(brune, part, keep_b, got_b, _, result, value, sem):
    copies = []
    for r in range(2):
        for c in range(part.shape[0]):
            second = (keep_b[c] + got_b[c]) * brune[1, :1]
            value[r, c] = repack(part[c], second)[r]
        copies.append(
            pltpu.make_async_copy(value.at[r], result.at[1, r], sem.at[r])
        )
        copies[r].start()
    for copy in copies:
        copy.wait()


def finish_last(brune, part, keep_b, got_b, result):
    return pl.pallas_call(
        finish_last_kernel,
        out_shape=jax.ShapeDtypeStruct(result.shape, result.dtype),
        in_specs=[VMEM_SPEC] * 4 + [HBM_SPEC],
        out_specs=HBM_SPEC,
        scratch_shapes=[
            pltpu.VMEM(result.shape[1:], result.dtype),
            pltpu.SemaphoreType.DMA((2,)),
        ],
        input_output_aliases={4: 0},
        compiler_params=pltpu.CompilerParams(vmem_limit_bytes=VMEM_LIMIT),
        cost_estimate=pl.CostEstimate(
            flops=400_000, bytes_accessed=600_000, transcendentals=0
        ),
    )(brune, part, keep_b, got_b, result)


def after(value, *others):
    return lax.optimization_barrier((value, *others))[0]


PAIRS = [(0, 1), (1, 0), (2, 3), (3, 2)]
INNER = [(1, 2), (2, 1)]
OUTER = [(1, 0), (2, 3)]


def line_steps(own, dense, table):
    move = functools.partial(lax.ppermute, axis_name="site")
    pairs = move(own, perm=PAIRS)
    inner = [move(own[0], perm=INNER), move(after(own, table)[1], perm=INNER)]
    outer = [move(inner[f], perm=OUTER) for f in range(FREQS)]
    ready = after(pairs, dense)
    acc = early(dense, own, pairs)
    middle = [
        move(after(ready[0], inner[0]), perm=INNER),
        move(after(ready[1], *inner, acc), perm=INNER),
    ]
    sums = [third(f, dense, acc, inner[f], outer[f]) for f in range(FREQS)]
    far0 = move(after(middle[0], sums[0]), perm=OUTER)
    width = own.shape[3] // 2
    handed = after(middle[1], sums[1])
    far1 = [
        move(handed[:, :, h * width : (h + 1) * width], perm=OUTER) for h in range(2)
    ]
    return sums, middle, far0, far1


def exchange(send):
    return lax.ppermute(send, "sub", [(0, 1), (1, 0)])


def shards(n_site, n_sub, tensor, spectra, pair_site, pair_block, pair_count, offset):
    spectra = spectra.transpose(0, 1, 3, 2, 4)
    tensor = tensor[0, 0, :, 0].transpose(0, 1, 2, 4, 3, 5)
    swap = n_sub == 2
    line = swap and n_site == SUB_BLOCKS
    half = lax.axis_index("sub") if swap else 0
    ids = jnp.stack([lax.axis_index("site"), half, lax.axis_index("var")])
    ids = jnp.pad(ids.astype(jnp.int32), (0, tensor.shape[0] - 3))
    table = jnp.stack([pair_site[0, 0], pair_block[0, 0], pair_count[0, 0], ids])
    freq_index = (offset[0] + jnp.arange(FREQS, dtype=jnp.int32)).astype(jnp.float32)
    brune = 1.0 / (1.0 + (freq_index / CORNER) ** 2)
    rows = jnp.broadcast_to(brune[:, None, None], (FREQS, 8, spectra.shape[3]))
    other = lax.ppermute(tensor, "var", [(0, 1), (1, 0)])
    dense = prepare(line, table, tensor, other)
    if line:
        sums, middle, far0, far1 = line_steps(spectra, dense, table)
        pieces = fourth(dense, sums[0], middle[0], far0)
        pieces = (pieces[0], exchange(pieces[1]))
        keep_a, send_a = last(0, dense, sums[1], middle[1], far1[0])
        got_a = exchange(send_a)
        final = after(far1[1], pieces[1], keep_a)
        keep_b, send_b = last(1, dense, sums[1], middle[1], final)
        got_b = exchange(send_b)
        result, part = finish_first(rows, *pieces, keep_a, got_a)
        result = finish_last(rows, part, keep_b, got_b, result)
    else:
        gathered = lax.all_gather(spectra, "site", axis=4, tiled=True)
        pieces = []
        for f in range(FREQS):
            blocks = gathered[f].reshape(gathered.shape[1:4] + (SUB_BLOCKS, -1))
            keep, send = whole(f, dense, blocks.transpose(3, 0, 1, 2, 4))
            if swap:
                pieces += [keep, exchange(send)]
            else:
                both = jnp.concatenate([keep, send], axis=2)
                keep = lax.psum_scatter(both, "sub", scatter_dimension=2, tiled=True)
                pieces += [keep, jnp.zeros_like(keep)]
        result = finish(rows, pieces)
    return result.transpose(0, 1, 2, 4, 3)


def solution(mesh):
    return jax.shard_map(
        functools.partial(shards, mesh.shape["site"], mesh.shape["sub"]),
        mesh=mesh,
        in_specs=(
            P(("scen", "site"), "sub", None, "var", None, None, None, None, None),
            P(None, None, ("scen", "var"), None, ("sub", "site")),
            P(("scen", "site"), "sub", None),
            P(("scen", "site"), "sub", None),
            P(("scen", "site"), "sub", None),
            P("scen"),
        ),
        out_specs=P(None, None, None, "var", ("scen", "site", "sub")),
        check_vma=False,
    )
```

```python
import functools

import jax
import jax.numpy as jnp
from jax import lax
from jax.experimental import pallas as pl
from jax.experimental.pallas import tpu as pltpu
from jax.sharding import PartitionSpec as P

FREQS = 2
SITE_BLOCKS = 4
SUB_BLOCKS = 4
CORNER = 48.0
VMEM_LIMIT = 40 << 20
PREPARE_LIMIT = 50 << 20

SMEM_SPEC = pl.BlockSpec(memory_space=pltpu.SMEM)
VMEM_SPEC = pl.BlockSpec(memory_space=pltpu.VMEM)
HBM_SPEC = pl.BlockSpec(memory_space=pl.ANY)


def place_of(block, z):
    flip = z >= 2
    block = jnp.where(flip, 3 - block, block)
    z = jnp.where(flip, 3 - z, z)
    return jnp.where(block < 2, block ^ z, block)


def prepare_kernel(line, table, own, other, dense, tiles, slot_of, counts, sem):
    z, j, v = table[3, 0], table[3, 1], table[3, 2]
    slots = own.shape[0]
    half = SITE_BLOCKS // 2
    _, _, comps, moments, block_sites, columns = own.shape

    def clear(i, _):
        slot_of[i] = 0
        counts[i] = 0
        return 0

    lax.fori_loop(0, SUB_BLOCKS * SITE_BLOCKS, clear, 0)

    def load(p, _):
        @pl.when(table[2, p] > 0)
        def _():
            pltpu.make_async_copy(own.at[p], tiles.at[0, p], sem).start()
            pltpu.make_async_copy(other.at[p], tiles.at[1, p], sem).start()
            block = table[1, p]
            place = place_of(block, z) if line else block
            s = table[0, p]
            at = place * SITE_BLOCKS + (s // half ^ j) * half + s % half
            slot_of[at] = p
            counts[at] = table[2, p]

        return 0

    lax.fori_loop(0, slots, load, 0)

    def drain(p, _):
        @pl.when(table[2, p] > 0)
        def _():
            pltpu.make_async_copy(own.at[p], tiles.at[0, p], sem).wait()
            pltpu.make_async_copy(other.at[p], tiles.at[1, p], sem).wait()

        return 0

    lax.fori_loop(0, slots, drain, 0)
    lane = lax.broadcasted_iota(jnp.int32, (block_sites, columns), 1)

    def lay(i, _):
        place = i // SITE_BLOCKS
        row = i % SITE_BLOCKS
        slot = slot_of[i]
        live = lane < counts[i]
        for role in range(2):
            f = v if role == 0 else 1 - v
            for r in range(2):
                start = pl.multiple_of((r * SITE_BLOCKS + row) * block_sites, block_sites)
                for c in range(comps):
                    for m in range(moments):
                        value = jnp.where(
                            live, tiles[role, slot, r, c, m], jnp.zeros((), dense.dtype)
                        )
                        dense[
                            f,
                            place,
                            c,
                            pl.ds(start, block_sites),
                            columns * m : columns * (m + 1),
                        ] = value
        return 0

    lax.fori_loop(0, SUB_BLOCKS * SITE_BLOCKS, lay, 0)


def prepare(line, table, own, other):
    slots, _, comps, moments, block_sites, columns = own.shape
    return pl.pallas_call(
        functools.partial(prepare_kernel, line),
        out_shape=pltpu.VMEM(
            (
                FREQS,
                SUB_BLOCKS,
                comps,
                2 * SITE_BLOCKS * block_sites,
                moments * columns,
            ),
            own.dtype,
        ),
        in_specs=[SMEM_SPEC] + [HBM_SPEC] * 2,
        out_specs=VMEM_SPEC,
        scratch_shapes=[
            pltpu.VMEM((2,) + own.shape, own.dtype),
            pltpu.SMEM((SUB_BLOCKS * SITE_BLOCKS,), jnp.int32),
            pltpu.SMEM((SUB_BLOCKS * SITE_BLOCKS,), jnp.int32),
            pltpu.SemaphoreType.DMA,
        ],
        compiler_params=pltpu.CompilerParams(vmem_limit_bytes=PREPARE_LIMIT),
        cost_estimate=pl.CostEstimate(
            flops=0, bytes_accessed=12_000_000, transcendentals=0
        ),
    )(table, own, other)


def products(dense, f, place, c, spectrum):
    moments, variants, columns = spectrum.shape[1:]
    rhs = jnp.concatenate(
        [spectrum[:, m].reshape(2 * variants, columns) for m in range(moments)], axis=1
    )
    total = lax.dot_general(
        dense[f, place, c],
        rhs,
        (((1,), (1,)), ((), ())),
        preferred_element_type=jnp.float32,
    )
    rows = total.shape[0] // 2
    real = total[:rows, :variants] - total[rows:, variants:]
    imag = total[:rows, variants:] + total[rows:, :variants]
    return real, imag


def early_kernel(dense, own, pairs, acc, spec, sem):
    copies = [
        pltpu.make_async_copy(source, spec.at[n], sem.at[n])
        for n, source in enumerate((own, pairs))
    ]
    for copy in copies:
        copy.start()
    for place in range(2):
        copies[place].wait()
        for f in range(FREQS):
            for c in range(dense.shape[2]):
                for r, value in enumerate(products(dense, f, place, c, spec[place, f])):
                    if place == 0:
                        acc[f, r, c] = value
                    else:
                        acc[f, r, c] += value


def early(dense, own, pairs):
    _, _, comps, rows, depth = dense.shape
    variants = own.shape[3]
    return pl.pallas_call(
        early_kernel,
        out_shape=pltpu.VMEM((FREQS, 2, comps, rows // 2, variants), jnp.float32),
        in_specs=[VMEM_SPEC, HBM_SPEC, HBM_SPEC],
        out_specs=VMEM_SPEC,
        scratch_shapes=[
            pltpu.VMEM((2,) + own.shape, own.dtype),
            pltpu.SemaphoreType.DMA((2,)),
        ],
        compiler_params=pltpu.CompilerParams(vmem_limit_bytes=VMEM_LIMIT),
        cost_estimate=pl.CostEstimate(
            flops=8 * comps * rows * 2 * variants * depth,
            bytes_accessed=4_000_000,
            transcendentals=0,
        ),
    )(dense, own, pairs)


def place_sums(dense, f, place, c, spectrum, sums):
    pair = products(dense, f, place, c, spectrum)
    return pair if sums is None else [a + b for a, b in zip(sums, pair)]


def swap_lanes(value):
    return pltpu.roll(value, value.shape[1] // 2, axis=1)


def low_lanes(value):
    lane = lax.broadcasted_iota(jnp.int32, value.shape, 1)
    return lane < value.shape[1] // 2


def repack(first, second):
    low = low_lanes(first)
    return (
        jnp.where(low, first, swap_lanes(second)),
        jnp.where(low, swap_lanes(first), second),
    )


def split_halves(sums, c, keep, send):
    half = keep.shape[2]
    for r, value in enumerate(sums):
        keep[r, c] = value[:half]
        send[r, c] = value[half:]


def by_position(run, middle, end):
    z = lax.axis_index("site")
    is_mid = jnp.logical_and(z > 0, z < 3)

    @pl.when(is_mid)
    def _():
        run(middle)

    @pl.when(jnp.logical_not(is_mid))
    def _():
        run(end)


def third_kernel(f, dense, acc, inner, outer, total):
    def run(source):
        for c in range(dense.shape[2]):
            sums = [acc[f, r, c] for r in range(2)]
            sums = place_sums(dense, f, 2, c, source[...], sums)
            for n, value in enumerate(sums if f == 0 else repack(*sums)):
                total[n, c] = value

    by_position(run, inner, outer)


def third(f, dense, acc, inner, outer):
    _, _, comps, rows, depth = dense.shape
    variants = inner.shape[2]
    return pl.pallas_call(
        functools.partial(third_kernel, f),
        out_shape=pltpu.VMEM((2, comps, rows // 2, variants), jnp.float32),
        in_specs=[VMEM_SPEC] * 4,
        out_specs=VMEM_SPEC,
        compiler_params=pltpu.CompilerParams(vmem_limit_bytes=VMEM_LIMIT),
        cost_estimate=pl.CostEstimate(
            flops=2 * comps * rows * 2 * variants * depth,
            bytes_accessed=1_000_000,
            transcendentals=0,
        ),
    )(dense, acc, inner, outer)


def fourth_kernel(dense, acc, middle, far, keep, send):
    def run(source):
        for c in range(dense.shape[2]):
            sums = [acc[r, c] for r in range(2)]
            split_halves(place_sums(dense, 0, 3, c, source[...], sums), c, keep, send)

    by_position(run, middle, far)


def fourth(dense, acc, middle, far):
    _, _, comps, rows, depth = dense.shape
    half = (2, comps, rows // 4, middle.shape[2])
    return pl.pallas_call(
        fourth_kernel,
        out_shape=(pltpu.VMEM(half, jnp.float32),) * 2,
        in_specs=[VMEM_SPEC] * 4,
        out_specs=(VMEM_SPEC,) * 2,
        compiler_params=pltpu.CompilerParams(vmem_limit_bytes=VMEM_LIMIT),
        cost_estimate=pl.CostEstimate(
            flops=2 * comps * rows * 2 * middle.shape[2] * depth,
            bytes_accessed=1_000_000,
            transcendentals=0,
        ),
    )(dense, acc, middle, far)


def last_kernel(h, sent, dense, acc, middle, far, out):
    moments, width, columns = far.shape[1:]
    half = out.shape[1]
    low = half if sent else 0

    def run(source):
        at = h * width if source is middle else 0
        rhs = jnp.concatenate(
            [
                source[:, m, at : at + width].reshape(2 * width, columns)
                for m in range(moments)
            ],
            axis=1,
        )
        for c in range(dense.shape[2]):
            lhs = jnp.concatenate(
                [
                    dense[1, 3, c, low + 2 * half * r : low + 2 * half * r + half]
                    for r in range(2)
                ],
                axis=0,
            )
            total = lax.dot_general(
                lhs, rhs, (((1,), (1,)), ((), ())), preferred_element_type=jnp.float32
            )
            crossed = swap_lanes(total[half:])
            crossed = jnp.where(low_lanes(crossed), -crossed, crossed)
            out[c] = acc[h, c, low : low + half] + (total[:half] + crossed)

    by_position(run, middle, far)


def last(h, sent, dense, acc, middle, far):
    _, _, comps, rows, depth = dense.shape
    half = (comps, rows // 4, 2 * far.shape[2])
    return pl.pallas_call(
        functools.partial(last_kernel, h, sent),
        out_shape=pltpu.VMEM(half, jnp.float32),
        in_specs=[VMEM_SPEC] * 4,
        out_specs=VMEM_SPEC,
        compiler_params=pltpu.CompilerParams(vmem_limit_bytes=VMEM_LIMIT),
        cost_estimate=pl.CostEstimate(
            flops=comps * rows * half[2] * depth,
            bytes_accessed=500_000,
            transcendentals=0,
        ),
    )(dense, acc, middle, far)


def whole_kernel(f, dense, parts, keep, send, spec, sem):
    copy = pltpu.make_async_copy(parts, spec, sem)
    copy.start()
    copy.wait()
    for c in range(dense.shape[2]):
        sums = None
        for place in range(SUB_BLOCKS):
            sums = place_sums(dense, f, place, c, spec[place], sums)
        split_halves(sums, c, keep, send)


def whole(f, dense, parts):
    _, _, comps, rows, depth = dense.shape
    half = jax.ShapeDtypeStruct((2, comps, rows // 4, parts.shape[3]), jnp.float32)
    return pl.pallas_call(
        functools.partial(whole_kernel, f),
        out_shape=(half, half),
        in_specs=[VMEM_SPEC, HBM_SPEC],
        out_specs=(VMEM_SPEC,) * 2,
        scratch_shapes=[
            pltpu.VMEM(parts.shape, parts.dtype),
            pltpu.SemaphoreType.DMA,
        ],
        compiler_params=pltpu.CompilerParams(vmem_limit_bytes=VMEM_LIMIT),
    )(dense, parts)


def finish_kernel(brune, *refs):
    result, value, sem = refs[-3:]
    copies = []
    for f in range(FREQS):
        keep, got = refs[2 * f : 2 * f + 2]
        for r in range(2):
            value[f, r] = (keep[r] + got[r]) * brune[f, :1]
            copy = pltpu.make_async_copy(value.at[f, r], result.at[f, r], sem.at[f, r])
            copy.start()
            copies.append(copy)
    for copy in copies:
        copy.wait()


def finish(brune, pieces):
    shape = (FREQS,) + pieces[0].shape
    return pl.pallas_call(
        finish_kernel,
        out_shape=jax.ShapeDtypeStruct(shape, pieces[0].dtype),
        in_specs=[VMEM_SPEC] * (1 + len(pieces)),
        out_specs=HBM_SPEC,
        scratch_shapes=[
            pltpu.VMEM(shape, pieces[0].dtype),
            pltpu.SemaphoreType.DMA((FREQS, 2)),
        ],
        compiler_params=pltpu.CompilerParams(vmem_limit_bytes=VMEM_LIMIT),
        cost_estimate=pl.CostEstimate(
            flops=400_000, bytes_accessed=600_000, transcendentals=0
        ),
    )(brune, *pieces)


def finish_first_kernel(brune, keep, got, keep_a, got_a, result, part, value, sem):
    copies = []
    for r in range(2):
        value[r] = (keep[r] + got[r]) * brune[0, :1]
        copies.append(
            pltpu.make_async_copy(value.at[r], result.at[0, r], sem.at[r])
        )
        copies[r].start()
    part[...] = (keep_a[...] + got_a[...]) * brune[1, :1]
    for copy in copies:
        copy.wait()


def finish_first(brune, keep, got, keep_a, got_a):
    return pl.pallas_call(
        finish_first_kernel,
        out_shape=(
            jax.ShapeDtypeStruct((FREQS,) + keep.shape, keep.dtype),
            pltpu.VMEM(keep_a.shape, keep.dtype),
        ),
        in_specs=[VMEM_SPEC] * 5,
        out_specs=(HBM_SPEC, VMEM_SPEC),
        scratch_shapes=[
            pltpu.VMEM(keep.shape, keep.dtype),
            pltpu.SemaphoreType.DMA((2,)),
        ],
        compiler_params=pltpu.CompilerParams(vmem_limit_bytes=VMEM_LIMIT),
        cost_estimate=pl.CostEstimate(
            flops=400_000, bytes_accessed=8_000_000, transcendentals=0
        ),
    )(brune, keep, got, keep_a, got_a)


def finish_last_kernel(brune, part, keep_b, got_b, _, result, value, sem):
    copies = []
    for c in range(part.shape[0]):
        second = (keep_b[c] + got_b[c]) * brune[1, :1]
        for r, total in enumerate(repack(part[c], second)):
            value[r, c] = total
            copy = pltpu.make_async_copy(
                value.at[r, c], result.at[1, r, c], sem.at[r, c]
            )
            copy.start()
            copies.append(copy)
    for copy in copies:
        copy.wait()


def finish_last(brune, part, keep_b, got_b, result):
    return pl.pallas_call(
        finish_last_kernel,
        out_shape=jax.ShapeDtypeStruct(result.shape, result.dtype),
        in_specs=[VMEM_SPEC] * 4 + [HBM_SPEC],
        out_specs=HBM_SPEC,
        scratch_shapes=[
            pltpu.VMEM(result.shape[1:], result.dtype),
            pltpu.SemaphoreType.DMA((2, 3)),
        ],
        input_output_aliases={4: 0},
        compiler_params=pltpu.CompilerParams(vmem_limit_bytes=VMEM_LIMIT),
        cost_estimate=pl.CostEstimate(
            flops=400_000, bytes_accessed=600_000, transcendentals=0
        ),
    )(brune, part, keep_b, got_b, result)


def after(value, *others):
    return lax.optimization_barrier((value, *others))[0]


PAIRS = [(0, 1), (1, 0), (2, 3), (3, 2)]
INNER = [(1, 2), (2, 1)]
OUTER = [(1, 0), (2, 3)]


def line_steps(own, dense, table):
    move = functools.partial(lax.ppermute, axis_name="site")
    pairs = move(own, perm=PAIRS)
    inner = [move(own[0], perm=INNER), move(after(own, table)[1], perm=INNER)]
    outer = [move(inner[f], perm=OUTER) for f in range(FREQS)]
    ready = after(pairs, dense)
    acc = early(dense, own, pairs)
    middle = [
        move(ready[0], perm=INNER),
        move(after(ready[1], *inner, acc), perm=INNER),
    ]
    sums = [third(f, dense, acc, inner[f], outer[f]) for f in range(FREQS)]
    far0 = move(after(middle[0], sums[0]), perm=OUTER)
    width = own.shape[3] // 2
    handed = after(middle[1], sums[1])
    far1 = [
        move(handed[:, :, h * width : (h + 1) * width], perm=OUTER) for h in range(2)
    ]
    return sums, middle, far0, far1


def exchange(send):
    return lax.ppermute(send, "sub", [(0, 1), (1, 0)])


def shards(n_site, n_sub, tensor, spectra, pair_site, pair_block, pair_count, offset):
    spectra = spectra.transpose(0, 1, 3, 2, 4)
    tensor = tensor[0, 0, :, 0].transpose(0, 1, 2, 4, 3, 5)
    swap = n_sub == 2
    line = swap and n_site == SUB_BLOCKS
    half = lax.axis_index("sub") if swap else 0
    ids = jnp.stack([lax.axis_index("site"), half, lax.axis_index("var")])
    ids = jnp.pad(ids.astype(jnp.int32), (0, tensor.shape[0] - 3))
    table = jnp.stack([pair_site[0, 0], pair_block[0, 0], pair_count[0, 0], ids])
    freq_index = (offset[0] + jnp.arange(FREQS, dtype=jnp.int32)).astype(jnp.float32)
    brune = 1.0 / (1.0 + (freq_index / CORNER) ** 2)
    rows = jnp.broadcast_to(brune[:, None, None], (FREQS, 8, spectra.shape[3]))
    other = lax.ppermute(tensor, "var", [(0, 1), (1, 0)])
    dense = prepare(line, table, tensor, other)
    if line:
        sums, middle, far0, far1 = line_steps(spectra, dense, table)
        pieces = fourth(dense, sums[0], middle[0], far0)
        pieces = (pieces[0], exchange(pieces[1]))
        shards_of = functools.partial(last, dense=dense, acc=sums[1], middle=middle[1])
        send_a = shards_of(0, True, far=far1[0])
        got_a = exchange(send_a)
        keep_a = shards_of(0, False, far=after(far1[0], send_a))
        final = after(far1[1], pieces[1], send_a)
        send_b = shards_of(1, True, far=final)
        got_b = exchange(send_b)
        keep_b = shards_of(1, False, far=after(final, send_b))
        result, part = finish_first(rows, *pieces, keep_a, got_a)
        result = finish_last(rows, part, keep_b, got_b, result)
    else:
        gathered = lax.all_gather(spectra, "site", axis=4, tiled=True)
        pieces = []
        for f in range(FREQS):
            blocks = gathered[f].reshape(gathered.shape[1:4] + (SUB_BLOCKS, -1))
            keep, send = whole(f, dense, blocks.transpose(3, 0, 1, 2, 4))
            if swap:
                pieces += [keep, exchange(send)]
            else:
                both = jnp.concatenate([keep, send], axis=2)
                keep = lax.psum_scatter(both, "sub", scatter_dimension=2, tiled=True)
                pieces += [keep, jnp.zeros_like(keep)]
        result = finish(rows, pieces)
    return result.transpose(0, 1, 2, 4, 3)


def solution(mesh):
    return jax.shard_map(
        functools.partial(shards, mesh.shape["site"], mesh.shape["sub"]),
        mesh=mesh,
        in_specs=(
            P(("scen", "site"), "sub", None, "var", None, None, None, None, None),
            P(None, None, ("scen", "var"), None, ("sub", "site")),
            P(("scen", "site"), "sub", None),
            P(("scen", "site"), "sub", None),
            P(("scen", "site"), "sub", None),
            P("scen"),
        ),
        out_specs=P(None, None, None, "var", ("scen", "site", "sub")),
        check_vma=False,
    )
```

```python
import functools

import jax
import jax.numpy as jnp
from jax import lax
from jax.experimental import pallas as pl
from jax.experimental.pallas import tpu as pltpu
from jax.sharding import PartitionSpec as P

FREQS = 2
SITE_BLOCKS = 4
SUB_BLOCKS = 4
CORNER = 48.0
VMEM_LIMIT = 40 << 20
PREPARE_LIMIT = 50 << 20

SMEM_SPEC = pl.BlockSpec(memory_space=pltpu.SMEM)
VMEM_SPEC = pl.BlockSpec(memory_space=pltpu.VMEM)
HBM_SPEC = pl.BlockSpec(memory_space=pl.ANY)


def place_of(block, z):
    flip = z >= 2
    block = jnp.where(flip, 3 - block, block)
    z = jnp.where(flip, 3 - z, z)
    return jnp.where(block < 2, block ^ z, block)


def prepare_kernel(line, table, own, other, dense, tiles, slot_of, counts, sem):
    z, j, v = table[3, 0], table[3, 1], table[3, 2]
    slots = own.shape[0]
    half = SITE_BLOCKS // 2
    _, _, comps, moments, block_sites, columns = own.shape

    def clear(i, _):
        slot_of[i] = 0
        counts[i] = 0
        return 0

    lax.fori_loop(0, SUB_BLOCKS * SITE_BLOCKS, clear, 0)

    def load(p, _):
        @pl.when(table[2, p] > 0)
        def _():
            pltpu.make_async_copy(own.at[p], tiles.at[0, p], sem).start()
            pltpu.make_async_copy(other.at[p], tiles.at[1, p], sem).start()
            block = table[1, p]
            place = place_of(block, z) if line else block
            s = table[0, p]
            at = place * SITE_BLOCKS + (s // half ^ j) * half + s % half
            slot_of[at] = p
            counts[at] = table[2, p]

        return 0

    lax.fori_loop(0, slots, load, 0)

    def drain(p, _):
        @pl.when(table[2, p] > 0)
        def _():
            pltpu.make_async_copy(own.at[p], tiles.at[0, p], sem).wait()
            pltpu.make_async_copy(other.at[p], tiles.at[1, p], sem).wait()

        return 0

    lax.fori_loop(0, slots, drain, 0)
    lane = lax.broadcasted_iota(jnp.int32, (block_sites, columns), 1)

    def lay(i, _):
        place = i // SITE_BLOCKS
        row = i % SITE_BLOCKS
        slot = slot_of[i]
        live = lane < counts[i]
        for role in range(2):
            f = v if role == 0 else 1 - v
            for r in range(2):
                start = pl.multiple_of((r * SITE_BLOCKS + row) * block_sites, block_sites)
                for c in range(comps):
                    for m in range(moments):
                        value = jnp.where(
                            live, tiles[role, slot, r, c, m], jnp.zeros((), dense.dtype)
                        )
                        dense[
                            f,
                            place,
                            c,
                            pl.ds(start, block_sites),
                            columns * m : columns * (m + 1),
                        ] = value
        return 0

    lax.fori_loop(0, SUB_BLOCKS * SITE_BLOCKS, lay, 0)


def prepare(line, table, own, other):
    slots, _, comps, moments, block_sites, columns = own.shape
    return pl.pallas_call(
        functools.partial(prepare_kernel, line),
        out_shape=pltpu.VMEM(
            (
                FREQS,
                SUB_BLOCKS,
                comps,
                2 * SITE_BLOCKS * block_sites,
                moments * columns,
            ),
            own.dtype,
        ),
        in_specs=[SMEM_SPEC] + [HBM_SPEC] * 2,
        out_specs=VMEM_SPEC,
        scratch_shapes=[
            pltpu.VMEM((2,) + own.shape, own.dtype),
            pltpu.SMEM((SUB_BLOCKS * SITE_BLOCKS,), jnp.int32),
            pltpu.SMEM((SUB_BLOCKS * SITE_BLOCKS,), jnp.int32),
            pltpu.SemaphoreType.DMA,
        ],
        compiler_params=pltpu.CompilerParams(vmem_limit_bytes=PREPARE_LIMIT),
        cost_estimate=pl.CostEstimate(
            flops=0, bytes_accessed=12_000_000, transcendentals=0
        ),
    )(table, own, other)


def products(dense, f, place, c, spectrum):
    moments, variants, columns = spectrum.shape[1:]
    rhs = jnp.concatenate(
        [spectrum[:, m].reshape(2 * variants, columns) for m in range(moments)], axis=1
    )
    total = lax.dot_general(
        dense[f, place, c],
        rhs,
        (((1,), (1,)), ((), ())),
        preferred_element_type=jnp.float32,
    )
    rows = total.shape[0] // 2
    real = total[:rows, :variants] - total[rows:, variants:]
    imag = total[:rows, variants:] + total[rows:, :variants]
    return real, imag


def early_kernel(dense, own, pairs, acc, spec, sem):
    copies = [
        pltpu.make_async_copy(source, spec.at[n], sem.at[n])
        for n, source in enumerate((own, pairs))
    ]
    for copy in copies:
        copy.start()
    for place in range(2):
        copies[place].wait()
        for f in range(FREQS):
            for c in range(dense.shape[2]):
                for r, value in enumerate(products(dense, f, place, c, spec[place, f])):
                    if place == 0:
                        acc[f, r, c] = value
                    else:
                        acc[f, r, c] += value


def early(dense, own, pairs):
    _, _, comps, rows, depth = dense.shape
    variants = own.shape[3]
    return pl.pallas_call(
        early_kernel,
        out_shape=pltpu.VMEM((FREQS, 2, comps, rows // 2, variants), jnp.float32),
        in_specs=[VMEM_SPEC, HBM_SPEC, HBM_SPEC],
        out_specs=VMEM_SPEC,
        scratch_shapes=[
            pltpu.VMEM((2,) + own.shape, own.dtype),
            pltpu.SemaphoreType.DMA((2,)),
        ],
        compiler_params=pltpu.CompilerParams(vmem_limit_bytes=VMEM_LIMIT),
        cost_estimate=pl.CostEstimate(
            flops=8 * comps * rows * 2 * variants * depth,
            bytes_accessed=4_000_000,
            transcendentals=0,
        ),
    )(dense, own, pairs)


def place_sums(dense, f, place, c, spectrum, sums):
    pair = products(dense, f, place, c, spectrum)
    return pair if sums is None else [a + b for a, b in zip(sums, pair)]


def swap_lanes(value):
    return pltpu.roll(value, value.shape[1] // 2, axis=1)


def low_lanes(value):
    lane = lax.broadcasted_iota(jnp.int32, value.shape, 1)
    return lane < value.shape[1] // 2


def repack(first, second):
    low = low_lanes(first)
    return (
        jnp.where(low, first, swap_lanes(second)),
        jnp.where(low, swap_lanes(first), second),
    )


def split_halves(sums, c, keep, send):
    half = keep.shape[2]
    for r, value in enumerate(sums):
        keep[r, c] = value[:half]
        send[r, c] = value[half:]


def by_position(run, middle, end):
    z = lax.axis_index("site")
    is_mid = jnp.logical_and(z > 0, z < 3)

    @pl.when(is_mid)
    def _():
        run(middle)

    @pl.when(jnp.logical_not(is_mid))
    def _():
        run(end)


def third_kernel(f, dense, acc, inner, outer, total):
    def run(source):
        for c in range(dense.shape[2]):
            sums = [acc[f, r, c] for r in range(2)]
            sums = place_sums(dense, f, 2, c, source[...], sums)
            for n, value in enumerate(sums if f == 0 else repack(*sums)):
                total[n, c] = value

    by_position(run, inner, outer)


def third(f, dense, acc, inner, outer):
    _, _, comps, rows, depth = dense.shape
    variants = inner.shape[2]
    return pl.pallas_call(
        functools.partial(third_kernel, f),
        out_shape=pltpu.VMEM((2, comps, rows // 2, variants), jnp.float32),
        in_specs=[VMEM_SPEC] * 4,
        out_specs=VMEM_SPEC,
        compiler_params=pltpu.CompilerParams(vmem_limit_bytes=VMEM_LIMIT),
        cost_estimate=pl.CostEstimate(
            flops=2 * comps * rows * 2 * variants * depth,
            bytes_accessed=1_000_000,
            transcendentals=0,
        ),
    )(dense, acc, inner, outer)


def fourth_kernel(dense, acc, middle, far, keep, send):
    def run(source):
        for c in range(dense.shape[2]):
            sums = [acc[r, c] for r in range(2)]
            split_halves(place_sums(dense, 0, 3, c, source[...], sums), c, keep, send)

    by_position(run, middle, far)


def fourth(dense, acc, middle, far):
    _, _, comps, rows, depth = dense.shape
    half = (2, comps, rows // 4, middle.shape[2])
    return pl.pallas_call(
        fourth_kernel,
        out_shape=(pltpu.VMEM(half, jnp.float32),) * 2,
        in_specs=[VMEM_SPEC] * 4,
        out_specs=(VMEM_SPEC,) * 2,
        compiler_params=pltpu.CompilerParams(vmem_limit_bytes=VMEM_LIMIT),
        cost_estimate=pl.CostEstimate(
            flops=2 * comps * rows * 2 * middle.shape[2] * depth,
            bytes_accessed=1_000_000,
            transcendentals=0,
        ),
    )(dense, acc, middle, far)


def last_kernel(h, sent, dense, acc, middle, far, out):
    moments, width, columns = far.shape[1:]
    half = out.shape[1]
    low = half if sent else 0

    def run(source):
        at = h * width if source is middle else 0
        rhs = jnp.concatenate(
            [
                source[:, m, at : at + width].reshape(2 * width, columns)
                for m in range(moments)
            ],
            axis=1,
        )
        for c in range(dense.shape[2]):
            lhs = jnp.concatenate(
                [
                    dense[1, 3, c, low + 2 * half * r : low + 2 * half * r + half]
                    for r in range(2)
                ],
                axis=0,
            )
            total = lax.dot_general(
                lhs, rhs, (((1,), (1,)), ((), ())), preferred_element_type=jnp.float32
            )
            crossed = swap_lanes(total[half:])
            crossed = jnp.where(low_lanes(crossed), -crossed, crossed)
            out[c] = acc[h, c, low : low + half] + (total[:half] + crossed)

    by_position(run, middle, far)


def last(h, sent, dense, acc, middle, far):
    _, _, comps, rows, depth = dense.shape
    half = (comps, rows // 4, 2 * far.shape[2])
    return pl.pallas_call(
        functools.partial(last_kernel, h, sent),
        out_shape=pltpu.VMEM(half, jnp.float32),
        in_specs=[VMEM_SPEC] * 4,
        out_specs=VMEM_SPEC,
        compiler_params=pltpu.CompilerParams(vmem_limit_bytes=VMEM_LIMIT),
        cost_estimate=pl.CostEstimate(
            flops=comps * rows * half[2] * depth,
            bytes_accessed=500_000,
            transcendentals=0,
        ),
    )(dense, acc, middle, far)


def whole_kernel(f, dense, parts, keep, send, spec, sem):
    copy = pltpu.make_async_copy(parts, spec, sem)
    copy.start()
    copy.wait()
    for c in range(dense.shape[2]):
        sums = None
        for place in range(SUB_BLOCKS):
            sums = place_sums(dense, f, place, c, spec[place], sums)
        split_halves(sums, c, keep, send)


def whole(f, dense, parts):
    _, _, comps, rows, depth = dense.shape
    half = jax.ShapeDtypeStruct((2, comps, rows // 4, parts.shape[3]), jnp.float32)
    return pl.pallas_call(
        functools.partial(whole_kernel, f),
        out_shape=(half, half),
        in_specs=[VMEM_SPEC, HBM_SPEC],
        out_specs=(VMEM_SPEC,) * 2,
        scratch_shapes=[
            pltpu.VMEM(parts.shape, parts.dtype),
            pltpu.SemaphoreType.DMA,
        ],
        compiler_params=pltpu.CompilerParams(vmem_limit_bytes=VMEM_LIMIT),
    )(dense, parts)


def finish_kernel(brune, *refs):
    result, value, sem = refs[-3:]
    copies = []
    for f in range(FREQS):
        keep, got = refs[2 * f : 2 * f + 2]
        for r in range(2):
            value[f, r] = (keep[r] + got[r]) * brune[f, :1]
            copy = pltpu.make_async_copy(value.at[f, r], result.at[f, r], sem.at[f, r])
            copy.start()
            copies.append(copy)
    for copy in copies:
        copy.wait()


def finish(brune, pieces):
    shape = (FREQS,) + pieces[0].shape
    return pl.pallas_call(
        finish_kernel,
        out_shape=jax.ShapeDtypeStruct(shape, pieces[0].dtype),
        in_specs=[VMEM_SPEC] * (1 + len(pieces)),
        out_specs=HBM_SPEC,
        scratch_shapes=[
            pltpu.VMEM(shape, pieces[0].dtype),
            pltpu.SemaphoreType.DMA((FREQS, 2)),
        ],
        compiler_params=pltpu.CompilerParams(vmem_limit_bytes=VMEM_LIMIT),
        cost_estimate=pl.CostEstimate(
            flops=400_000, bytes_accessed=600_000, transcendentals=0
        ),
    )(brune, *pieces)


def finish_first_kernel(brune, keep, got, keep_a, got_a, result, part, value, sem):
    copies = []
    for r in range(2):
        value[r] = (keep[r] + got[r]) * brune[0, :1]
        copies.append(
            pltpu.make_async_copy(value.at[r], result.at[0, r], sem.at[r])
        )
        copies[r].start()
    for c in range(keep_a.shape[0]):
        part[0, c] = (keep_a[c] + got_a[c]) * brune[1, :1]
        part[1, c] = swap_lanes(part[0, c])
    for copy in copies:
        copy.wait()


def finish_first(brune, keep, got, keep_a, got_a):
    return pl.pallas_call(
        finish_first_kernel,
        out_shape=(
            jax.ShapeDtypeStruct((FREQS,) + keep.shape, keep.dtype),
            pltpu.VMEM((2,) + keep_a.shape, keep.dtype),
        ),
        in_specs=[VMEM_SPEC] * 5,
        out_specs=(HBM_SPEC, VMEM_SPEC),
        scratch_shapes=[
            pltpu.VMEM(keep.shape, keep.dtype),
            pltpu.SemaphoreType.DMA((2,)),
        ],
        compiler_params=pltpu.CompilerParams(vmem_limit_bytes=VMEM_LIMIT),
        cost_estimate=pl.CostEstimate(
            flops=400_000, bytes_accessed=8_000_000, transcendentals=0
        ),
    )(brune, keep, got, keep_a, got_a)


def finish_last_kernel(brune, part, keep_b, got_b, _, result, value, sem):
    copies = []
    low = low_lanes(keep_b[0])
    for c in range(keep_b.shape[0]):
        second = (keep_b[c] + got_b[c]) * brune[1, :1]
        real = jnp.where(low, part[0, c], swap_lanes(second))
        for r, total in enumerate((real, jnp.where(low, part[1, c], second))):
            value[r, c] = total
            copy = pltpu.make_async_copy(
                value.at[r, c], result.at[1, r, c], sem.at[r, c]
            )
            copy.start()
            copies.append(copy)
    for copy in copies:
        copy.wait()


def finish_last(brune, part, keep_b, got_b, result):
    return pl.pallas_call(
        finish_last_kernel,
        out_shape=jax.ShapeDtypeStruct(result.shape, result.dtype),
        in_specs=[VMEM_SPEC] * 4 + [HBM_SPEC],
        out_specs=HBM_SPEC,
        scratch_shapes=[
            pltpu.VMEM(result.shape[1:], result.dtype),
            pltpu.SemaphoreType.DMA((2, 3)),
        ],
        input_output_aliases={4: 0},
        compiler_params=pltpu.CompilerParams(vmem_limit_bytes=VMEM_LIMIT),
        cost_estimate=pl.CostEstimate(
            flops=400_000, bytes_accessed=600_000, transcendentals=0
        ),
    )(brune, part, keep_b, got_b, result)


def after(value, *others):
    return lax.optimization_barrier((value, *others))[0]


PAIRS = [(0, 1), (1, 0), (2, 3), (3, 2)]
INNER = [(1, 2), (2, 1)]
OUTER = [(1, 0), (2, 3)]


def line_steps(own, dense, table):
    move = functools.partial(lax.ppermute, axis_name="site")
    pairs = move(own, perm=PAIRS)
    inner = [move(own[0], perm=INNER), move(after(own, table)[1], perm=INNER)]
    outer = [move(inner[f], perm=OUTER) for f in range(FREQS)]
    ready = after(pairs, dense)
    acc = early(dense, own, pairs)
    middle = [
        move(ready[0], perm=INNER),
        move(after(ready[1], *inner, acc), perm=INNER),
    ]
    sums = [third(f, dense, acc, inner[f], outer[f]) for f in range(FREQS)]
    far0 = move(after(middle[0], sums[0]), perm=OUTER)
    width = own.shape[3] // 2
    handed = after(middle[1], sums[1])
    far1 = [
        move(handed[:, :, h * width : (h + 1) * width], perm=OUTER) for h in range(2)
    ]
    return sums, middle, far0, far1


def exchange(send):
    return lax.ppermute(send, "sub", [(0, 1), (1, 0)])


def shards(n_site, n_sub, tensor, spectra, pair_site, pair_block, pair_count, offset):
    spectra = spectra.transpose(0, 1, 3, 2, 4)
    tensor = tensor[0, 0, :, 0].transpose(0, 1, 2, 4, 3, 5)
    swap = n_sub == 2
    line = swap and n_site == SUB_BLOCKS
    half = lax.axis_index("sub") if swap else 0
    ids = jnp.stack([lax.axis_index("site"), half, lax.axis_index("var")])
    ids = jnp.pad(ids.astype(jnp.int32), (0, tensor.shape[0] - 3))
    table = jnp.stack([pair_site[0, 0], pair_block[0, 0], pair_count[0, 0], ids])
    freq_index = (offset[0] + jnp.arange(FREQS, dtype=jnp.int32)).astype(jnp.float32)
    brune = 1.0 / (1.0 + (freq_index / CORNER) ** 2)
    rows = jnp.broadcast_to(brune[:, None, None], (FREQS, 8, spectra.shape[3]))
    other = lax.ppermute(tensor, "var", [(0, 1), (1, 0)])
    dense = prepare(line, table, tensor, other)
    if line:
        sums, middle, far0, far1 = line_steps(spectra, dense, table)
        pieces = fourth(dense, sums[0], middle[0], far0)
        pieces = (pieces[0], exchange(pieces[1]))
        shards_of = functools.partial(last, dense=dense, acc=sums[1], middle=middle[1])
        send_a = shards_of(0, True, far=far1[0])
        got_a = exchange(send_a)
        keep_a = shards_of(0, False, far=after(far1[0], send_a))
        final = after(far1[1], pieces[1], send_a)
        send_b = shards_of(1, True, far=final)
        got_b = exchange(send_b)
        keep_b = shards_of(1, False, far=after(final, send_b))
        result, part = finish_first(rows, *pieces, keep_a, got_a)
        result = finish_last(rows, part, keep_b, got_b, result)
    else:
        gathered = lax.all_gather(spectra, "site", axis=4, tiled=True)
        pieces = []
        for f in range(FREQS):
            blocks = gathered[f].reshape(gathered.shape[1:4] + (SUB_BLOCKS, -1))
            keep, send = whole(f, dense, blocks.transpose(3, 0, 1, 2, 4))
            if swap:
                pieces += [keep, exchange(send)]
            else:
                both = jnp.concatenate([keep, send], axis=2)
                keep = lax.psum_scatter(both, "sub", scatter_dimension=2, tiled=True)
                pieces += [keep, jnp.zeros_like(keep)]
        result = finish(rows, pieces)
    return result.transpose(0, 1, 2, 4, 3)


def solution(mesh):
    return jax.shard_map(
        functools.partial(shards, mesh.shape["site"], mesh.shape["sub"]),
        mesh=mesh,
        in_specs=(
            P(("scen", "site"), "sub", None, "var", None, None, None, None, None),
            P(None, None, ("scen", "var"), None, ("sub", "site")),
            P(("scen", "site"), "sub", None),
            P(("scen", "site"), "sub", None),
            P(("scen", "site"), "sub", None),
            P("scen"),
        ),
        out_specs=P(None, None, None, "var", ("scen", "site", "sub")),
        check_vma=False,
    )
```
